32 devices in a mesh: fsdp: 16 (over z, y, x), tp: 2 (over core).
Axes of the slice: x: 2, y: 2, z: 4, core: 2. Of those that a mesh axis runs over, the one named last changes fastest.
Arguments:
- owner: int32 [2, 7], replicated, may hold values from 0 to 15, as said below
- grads: bfloat16 [2, 896, 2, 8320], P(None, 'fsdp', 'tp')
- weights: float32 [2, 896, 2, 8320], P(None, 'fsdp', 'tp'), may hold values from -0.1875 to 0.1875
- adam_m: float32 [2, 896, 2, 8320], P(None, 'fsdp', 'tp'), may hold values from -0.4375 to 0.4375
- adam_v: float32 [2, 896, 2, 8320], P(None, 'fsdp', 'tp'), may hold values from 0.0001 to 0.1
- stats: float32 [16, 896, 896], P('fsdp', 'tp')
- roots: bfloat16 [16, 896, 896], P('fsdp', 'tp')
- vec_weight: float32 [2, 2944], P(None, ('fsdp', 'tp')), may hold values from 0.5 to 1.5
- vec_grad: bfloat16 [2, 2944], P(None, ('fsdp', 'tp')), may hold values from -1.5 to 1.5
- vec_m: float32 [2, 2944], P(None, ('fsdp', 'tp')), may hold values from -0.4375 to 0.4375
- vec_v: float32 [2, 2944], P(None, ('fsdp', 'tp')), may hold values from 0.0001 to 0.1
Outputs:
- weights_new: float32 [2, 896, 2, 8320], P(None, 'fsdp', 'tp')
- adam_m_new: float32 [2, 896, 2, 8320], P(None, 'fsdp', 'tp')
- adam_v_new: float32 [2, 896, 2, 8320], P(None, 'fsdp', 'tp')
- stats_new: float32 [16, 896, 896], P('fsdp', 'tp')
- vec_weight_new: float32 [2, 2944], P(None, ('fsdp', 'tp'))
- vec_m_new: float32 [2, 2944], P(None, ('fsdp', 'tp'))
- vec_v_new: float32 [2, 2944], P(None, ('fsdp', 'tp'))
The draws below stay inside these ranges and needn't reach their ends.
Inputs may be any that keep to these rules, and one draw needn't show every extreme that they name: owner[l, t] is the index along fsdp of the chip whose slot holds the statistic of kind t of layer l; all 14 values are distinct, so a chip owns at most one matrix and some chips own none.
All inputs are finite; a program needn't handle non-finite values.
Results may differ from the reference program's by a relative error of at most 0.0015.
Values may be sent and summed in bfloat16 or wider, within the bound.
No kernel may reach another device: no remote copies, remote signals or barrier semaphores. Data moves between devices by JAX's collectives and lax.ppermute only.
A program may use at most 192 MiB of HBM per device.

```python
import math
import jax
import jax.numpy as jnp

D = 896
FF = 4864
NL = 2
QW = 896
KW = 128
CH = 8320
VW = 2944
N_FSDP = 16


def draw_owner(key, part):
    chips = N_FSDP
    total = NL * 7
    middle = 1 + jax.random.permutation(jax.random.fold_in(key, 11), chips - 2)
    chosen = jnp.concatenate([jnp.array([0, chips - 1], jnp.int32), middle[:total - 2].astype(jnp.int32)])
    order = jax.random.permutation(jax.random.fold_in(key, 12), total)
    return chosen[order].reshape(NL, 7).astype(jnp.int32)


def draw_grads(key, part):
    shape = (NL, D, 2, CH)
    base = jax.random.normal(jax.random.fold_in(key, 21), shape, jnp.float32)
    rise = 3.0
    position = jnp.arange(D, dtype=jnp.float32) / (D - 1)
    row_rise = jnp.exp(math.log(rise) * position)[None, :, None, None]
    row_rand = jnp.exp(jax.random.uniform(jax.random.fold_in(key, 24), (NL, D, 1, 1), jnp.float32, math.log(0.3), math.log(3.0)))
    col_rand = jnp.exp(jax.random.uniform(jax.random.fold_in(key, 25), (NL, 1, 2, CH), jnp.float32, math.log(0.3), math.log(3.0)))
    return (0.1 * base * row_rise * row_rand * col_rand).astype(jnp.bfloat16)


def symmetric_draw(key, scale, low, high):
    shape = (N_FSDP, D, D)
    noise = jax.random.normal(jax.random.fold_in(key, 32), shape, jnp.float32)
    off_part = 0.5 * scale * (noise + jnp.swapaxes(noise, 1, 2))
    diagonal = jnp.exp(jax.random.uniform(jax.random.fold_in(key, 33), (N_FSDP, D, 1), jnp.float32, math.log(low), math.log(high)))
    identity = (jnp.arange(D)[:, None] == jnp.arange(D)[None, :]).astype(jnp.float32)
    return off_part * (1.0 - identity)[None] + diagonal * identity[None]


def draw_stats(key, part):
    return symmetric_draw(jax.random.fold_in(key, 41), 0.05, 0.5, 5.0)


def draw_roots(key, part):
    return symmetric_draw(jax.random.fold_in(key, 42), 0.5 / math.sqrt(D), 0.5, 2.0).astype(jnp.bfloat16)


def level_of(key, dims, cuts, smallest, largest):
    def one(dim, shards_of):
        steps = jax.random.uniform(jax.random.fold_in(jax.random.fold_in(key, 6), dim), (shards_of,), jnp.float32, smallest / len(cuts), largest / len(cuts))
        return jnp.repeat(jnp.exp(steps), dims[dim] // shards_of).reshape((-1,) + (1,) * (len(dims) - dim - 1))

    gain = one(*cuts[0])
    for cut in cuts[1:]:
        gain = gain * one(*cut)
    return gain


def bell_draw(rng, shape, scale, limit, cuts=(), held_as=jnp.bfloat16):
    level = level_of(rng, shape, cuts, -0.22, 0.18) if cuts else 1.0
    entries = jax.random.normal(rng, shape, jnp.float32) * scale * level
    return jnp.minimum(jnp.maximum(entries, -limit), limit).astype(held_as)


def setup_inputs(seed: int = 0) -> dict:
    streams_of = jax.random.split(jax.random.key(seed), 12)
    return {
        "owner": draw_owner(jax.random.fold_in(streams_of[11], 71), 0),
        "grads": draw_grads(jax.random.fold_in(streams_of[11], 71), 0),
        "weights": bell_draw(streams_of[2], (NL, D, 2, CH), D ** -0.5, 0.1875, ((1, 16), (2, 2)), jnp.float32),
        "adam_m": bell_draw(streams_of[3], (NL, D, 2, CH), 0.03, 0.4375, ((1, 16), (2, 2)), jnp.float32),
        "adam_v": jnp.clip(jnp.exp(math.log(0.1) - 6.9077553 * jax.random.uniform(streams_of[4], (NL, D, 2, CH), jnp.float32) ** level_of(streams_of[4], (NL, D, 2, CH), ((1, 16), (2, 2)), -0.2, 0.2)), 0.0001, 0.1),
        "stats": draw_stats(jax.random.fold_in(streams_of[11], 71), 0),
        "roots": draw_roots(jax.random.fold_in(streams_of[11], 71), 0),
        "vec_weight": jnp.clip(1.0 + 0.1 * jax.random.normal(streams_of[7], (NL, VW), jnp.float32), 0.5, 1.5),
        "vec_grad": bell_draw(streams_of[8], (NL, VW), 0.1, 1.5, ((1, 32),)),
        "vec_m": bell_draw(streams_of[9], (NL, VW), 0.03, 0.4375, ((1, 32),), jnp.float32),
        "vec_v": jnp.clip(jnp.exp(math.log(0.1) - 6.9077553 * jax.random.uniform(streams_of[10], (NL, VW), jnp.float32) ** level_of(streams_of[10], (NL, VW), ((1, 32),), -0.2, 0.2)), 0.0001, 0.1),
    }


def half_widths():
    return [QW // 2, KW // 2, KW // 2, QW // 2, FF // 2, FF // 2, FF // 2]

def column_starts(widths):
    starts = []
    position = 0
    for wide in widths:
        starts.append(position)
        position = position + wide
    return starts

def reference(owner, grads, weights, adam_m, adam_v, stats, roots, vec_weight, vec_grad, vec_m, vec_v):
    widths = half_widths()
    starts = column_starts(widths)
    grad_float = grads.astype(jnp.float32)
    adam_m_new = 0.9 * adam_m + 0.1 * grad_float
    adam_v_new = 0.99 * adam_v + 0.01 * grad_float * grad_float
    adam_step = adam_m_new / (jnp.sqrt(adam_v_new) + 1e-08)
    stats_new = stats
    layers = grads.shape[0]
    blocks = []
    for layer in range(layers):
        pieces = []
        for kind in range(7):
            first = starts[kind]
            wide = widths[kind]
            matrix = jnp.concatenate([grads[layer, :, 0, first:first + wide], grads[layer, :, 1, first:first + wide]], axis=1)
            slot = owner[layer, kind]
            gram = jnp.dot(matrix, matrix.T, preferred_element_type=jnp.float32)
            stats_new = stats_new.at[slot].set(0.9 * stats[slot] + 0.1 * gram)
            precon = jnp.dot(roots[slot], matrix, preferred_element_type=jnp.float32).astype(jnp.bfloat16)
            precon_float = precon.astype(jnp.float32)
            adam_piece = adam_step[layer, :, :, first:first + wide]
            ratio = jnp.sqrt(jnp.sum(adam_piece * adam_piece)) / (jnp.sqrt(jnp.sum(precon_float * precon_float)) + 1e-06)
            scaled = ratio * precon_float
            pieces.append(jnp.stack([scaled[:, :wide], scaled[:, wide:]], axis=1))
        blocks.append(jnp.concatenate(pieces, axis=2))
    update = jnp.stack(blocks, axis=0)
    weights_new = weights - 0.02 * update
    vec_float = vec_grad.astype(jnp.float32)
    vec_m_new = 0.9 * vec_m + 0.1 * vec_float
    vec_v_new = 0.99 * vec_v + 0.01 * vec_float * vec_float
    vec_weight_new = vec_weight - 0.02 * vec_m_new / (jnp.sqrt(vec_v_new) + 1e-08)
    return (weights_new, adam_m_new, adam_v_new, stats_new, vec_weight_new, vec_m_new, vec_v_new)
```

```python
import jax
import jax.numpy as jnp
from jax import lax
from jax.experimental import pallas as pl
from jax.experimental.pallas import tpu as pltpu
from jax.sharding import PartitionSpec as P

FF = 4864
QW = 896
KW = 128
LANES = 128
WIDTHS = [QW // 2, KW // 2, KW // 2, QW // 2, FF // 2, FF // 2, FF // 2]
STARTS = [sum(WIDTHS[:kind]) for kind in range(7)]
TILE0 = [start // LANES for start in STARTS]
TILES = [-(-(start + wide) // LANES) - start // LANES for start, wide in zip(STARTS, WIDTHS)]
CAP = max(TILES)
HALF = sum(WIDTHS)
ALL_TILES = HALF // LANES


def row_block(rows):
    return 8 if rows % 8 == 0 else rows


def send_kernel(layer_ref, tile_ref, low_ref, high_ref, grad_ref, out_ref):
    slot = pl.program_id(0)
    layer = layer_ref[slot]
    first = tile_ref[slot]
    low = low_ref[slot]
    high = high_ref[slot]
    lane = lax.broadcasted_iota(jnp.int32, (grad_ref.shape[1], LANES), 1)
    for tile in range(CAP):
        at = jnp.minimum(first + tile, ALL_TILES - 1)
        piece = grad_ref[layer, :, pl.ds(pl.multiple_of(at * LANES, LANES), LANES)]
        column = lane + (first + tile) * LANES
        keep = (column >= low) & (column < high)
        out_ref[0, :, tile * LANES : (tile + 1) * LANES] = jnp.where(
            keep, piece.astype(jnp.float32), 0.0
        ).astype(jnp.bfloat16)


def build_send(grads, slot_layer, slot_kind):
    layers, rows, _ = grads.shape
    chips = slot_layer.shape[0]
    tile0 = jnp.array(TILE0 + [0], jnp.int32)[slot_kind]
    low = jnp.array(STARTS + [0], jnp.int32)[slot_kind]
    high = jnp.array([s + w for s, w in zip(STARTS, WIDTHS)] + [0], jnp.int32)[slot_kind]
    return pl.pallas_call(
        send_kernel,
        out_shape=jax.ShapeDtypeStruct((chips, rows, CAP * LANES), jnp.bfloat16),
        grid_spec=pltpu.PrefetchScalarGridSpec(
            num_scalar_prefetch=4,
            grid=(chips,),
            in_specs=[pl.BlockSpec((layers, rows, HALF), lambda i, *_: (0, 0, 0))],
            out_specs=pl.BlockSpec((1, rows, CAP * LANES), lambda i, *_: (i, 0, 0)),
        ),
        name="build_send",
    )(slot_layer, tile0, low, high, grads)


def update_kernel(owner_ref, scale_ref, weight_ref, *refs):
    pieces = refs[:7]
    out_ref = refs[7]
    layer = pl.program_id(0)
    rows = pieces[0].shape[1]
    lane = lax.broadcasted_iota(jnp.int32, (rows, LANES), 1)
    for tile in range(ALL_TILES):
        step = None
        for kind in range(7):
            at = tile - TILE0[kind]
            if not 0 <= at < TILES[kind]:
                continue
            piece = pieces[kind][0, :, at * LANES : (at + 1) * LANES].astype(jnp.float32)
            piece = 0.02 * (scale_ref[layer, kind] * piece)
            low = STARTS[kind] - tile * LANES
            if step is not None:
                step = jnp.where(lane >= low, piece, step)
            else:
                step = piece
        where = pl.ds(tile, rows, stride=ALL_TILES)
        out_ref[0, where, :] = weight_ref[0, where, :] - step


def update_weights(owner, ratio, weights, returned):
    layers, rows = weights.shape[:2]
    block = row_block(rows)
    blocks = rows // block
    view = (layers * blocks, block * ALL_TILES, LANES)

    def piece_spec(kind):
        wide = TILES[kind] * LANES
        return pl.BlockSpec((1, block, wide), lambda l, r, owner, scale: (owner[l, kind], r, 0))

    flat_spec = pl.BlockSpec((1,) + view[1:], lambda l, r, owner, scale: (l * blocks + r, 0, 0))
    out = pl.pallas_call(
        update_kernel,
        out_shape=jax.ShapeDtypeStruct(view, jnp.float32),
        grid_spec=pltpu.PrefetchScalarGridSpec(
            num_scalar_prefetch=2,
            grid=(layers, blocks),
            in_specs=[flat_spec] + [piece_spec(kind) for kind in range(7)],
            out_specs=flat_spec,
        ),
        name="update_weights",
    )(owner, ratio, weights.reshape(view), *[returned] * 7)
    return out.reshape(weights.shape)


def kind_sums(values):
    return jnp.stack(
        [
            jnp.sum(values[:, :, start : start + wide], axis=(1, 2))
            for start, wide in zip(STARTS, WIDTHS)
        ],
        axis=1,
    )


def swap_cores(value):
    return lax.ppermute(value, "tp", [(0, 1), (1, 0)])


def on_device(
    owner, grads, weights, adam_m, adam_v, stats, roots, vec_weight, vec_grad, vec_m, vec_v
):
    chips = lax.axis_size("fsdp")
    chip = lax.axis_index("fsdp")
    core = lax.axis_index("tp")
    layers = grads.shape[0]
    rows = grads.shape[1]
    model_rows = rows * chips
    half_rows = model_rows // 2
    flat_owner = owner.reshape(-1)
    named = flat_owner[None, :] == jnp.arange(chips, dtype=jnp.int32)[:, None]
    order = jnp.arange(layers * 7, dtype=jnp.int32)[None, :]
    matrix = jnp.sum(jnp.where(named, order, 0), axis=1)
    has = jnp.any(named, axis=1)
    slot_layer = matrix // 7
    slot_kind = jnp.where(has, matrix % 7, 7)
    owned = has[chip]

    outgoing = build_send(grads[:, :, 0, :], slot_layer, slot_kind)
    arrived = lax.all_to_all(outgoing, "fsdp", split_axis=0, concat_axis=0, tiled=True)
    gathered = arrived.reshape(model_rows, CAP * LANES)

    root_mine = roots[0]
    root_other = swap_cores(root_mine)
    root = jnp.where(
        core == 0,
        jnp.concatenate([root_mine, root_other]),
        jnp.concatenate([root_other, root_mine]),
    )

    grad_float = grads.astype(jnp.float32)
    adam_m_new = 0.9 * adam_m + 0.1 * grad_float
    adam_v_new = 0.99 * adam_v + 0.01 * grad_float * grad_float
    adam_step = (adam_m_new / (jnp.sqrt(adam_v_new) + 1e-08))[:, :, 0, :]
    adam_part = kind_sums(adam_step * adam_step)

    precond = jnp.dot(root, gathered, preferred_element_type=jnp.float32).astype(jnp.bfloat16)
    returned = lax.all_to_all(
        precond.reshape(chips, rows, CAP * LANES), "fsdp", split_axis=0, concat_axis=0, tiled=True
    )
    precond_float = precond.astype(jnp.float32)
    shampoo_part = jnp.sum(precond_float * precond_float)
    mine = jnp.where(named[chip], shampoo_part, 0.0).reshape(layers, 7)
    adam_total, shampoo_total = lax.psum((adam_part, mine), ("fsdp", "tp"))
    ratio = jnp.sqrt(adam_total) / (jnp.sqrt(shampoo_total) + 1e-06)

    gram = lax.dot_general(
        gathered, gathered, (((1,), (1,)), ((), ())), preferred_element_type=jnp.float32
    )
    top = gram[:half_rows]
    bottom = gram[half_rows:]
    keep = jnp.where(core == 0, top, bottom)
    give = jnp.where(core == 0, bottom, top)
    stat_term = keep + swap_cores(give)
    stats_new = jnp.where(owned, 0.9 * stats[0] + 0.1 * stat_term, stats[0])[None]

    weights_new = update_weights(owner, ratio, weights, returned)

    vec_float = vec_grad.astype(jnp.float32)
    vec_m_new = 0.9 * vec_m + 0.1 * vec_float
    vec_v_new = 0.99 * vec_v + 0.01 * vec_float * vec_float
    vec_weight_new = vec_weight - 0.02 * vec_m_new / (jnp.sqrt(vec_v_new) + 1e-08)
    return (weights_new, adam_m_new, adam_v_new, stats_new, vec_weight_new, vec_m_new, vec_v_new)


def solution(mesh):
    matrix = P(None, "fsdp", "tp", None)
    slot = P("fsdp", "tp", None)
    vector = P(None, ("fsdp", "tp"))
    return jax.shard_map(
        on_device,
        mesh=mesh,
        in_specs=(P(), matrix, matrix, matrix, matrix, slot, slot, vector, vector, vector, vector),
        out_specs=(matrix, matrix, matrix, slot, vector, vector, vector),
        check_vma=False,
    )
```

```python
import functools

import jax
import jax.numpy as jnp
from jax import lax
from jax.experimental import pallas as pl
from jax.experimental.pallas import tpu as pltpu
from jax.sharding import PartitionSpec as P

FF = 4864
QW = 896
KW = 128
LANES = 128
WIDTHS = [QW // 2, KW // 2, KW // 2, QW // 2, FF // 2, FF // 2, FF // 2]
STARTS = [sum(WIDTHS[:kind]) for kind in range(7)]
TILE0 = [start // LANES for start in STARTS]
TILES = [-(-(start + wide) // LANES) - start // LANES for start, wide in zip(STARTS, WIDTHS)]
HALF = sum(WIDTHS)
ALL_TILES = HALF // LANES
GROUP = 4
WIDE = -(-max(TILES) // GROUP)
FIRST_WIDE = 4
NONE = 7


def pick(index, values):
    result = jnp.int32(values[-1])
    for at in range(len(values) - 1):
        result = jnp.where(index == at, values[at], result)
    return result


def rank_tile(rank, wide_ranks):
    return jnp.where(rank < wide_ranks, rank * WIDE, wide_ranks * (WIDE - 1) + rank)


def slot_tiles(wide_ranks):
    return wide_ranks * WIDE + GROUP - wide_ranks


def plan_kernel(owner_ref, layer_ref, kind_ref, place_ref, base_ref, rank_ref, level_ref, mat_ref):
    layers = owner_ref.shape[0]
    chips = layer_ref.shape[0]

    def clear(chip, carry):
        mat_ref[chip] = -1
        return carry

    lax.fori_loop(0, chips, clear, 0)

    def name(matrix, carry):
        mat_ref[owner_ref[matrix // 7, matrix % 7]] = matrix
        return carry

    lax.fori_loop(0, layers * 7, name, 0)

    def rank_group(group, level):
        first = group * GROUP
        mats = [mat_ref[first + i] for i in range(GROUP)]
        wide = [((m >= 0) & (m % 7 >= FIRST_WIDE)).astype(jnp.int32) for m in mats]
        count = sum(wide)
        before_wide = jnp.int32(0)
        before_rest = count
        for i in range(GROUP):
            rank = jnp.where(wide[i] == 1, before_wide, before_rest)
            before_wide = before_wide + wide[i]
            before_rest = before_rest + 1 - wide[i]
            there = first + rank
            layer_ref[there] = jnp.maximum(mats[i], 0) // 7
            kind_ref[there] = jnp.where(mats[i] >= 0, jnp.maximum(mats[i], 0) % 7, NONE)
            place_ref[there] = i

            @pl.when(mats[i] >= 0)
            def _():
                base_ref[mats[i]] = first
                rank_ref[mats[i]] = rank

        return jnp.maximum(level, count)

    level_ref[0] = lax.fori_loop(0, chips // GROUP, rank_group, jnp.int32(0))


def make_plan(owner, chips):
    matrices = owner.shape[0] * 7
    sizes = [chips, chips, chips, matrices, matrices, 1]
    smem = pl.BlockSpec(memory_space=pltpu.SMEM)
    return pl.pallas_call(
        plan_kernel,
        out_shape=[jax.ShapeDtypeStruct((size,), jnp.int32) for size in sizes],
        in_specs=[smem],
        out_specs=[smem] * len(sizes),
        scratch_shapes=[pltpu.SMEM((chips,), jnp.int32)],
        name="plan",
    )(owner)


def send_kernel(wide_ranks, layer_ref, kind_ref, grad_ref, out_ref):
    slot = pl.program_id(0)
    part = slot % GROUP
    group = slot - part
    rows = grad_ref.shape[1]
    lane = lax.broadcasted_iota(jnp.int32, (rows, LANES), 1)
    blank = jnp.zeros((rows, LANES), jnp.bfloat16)

    def tile_of(layer, at):
        return grad_ref[layer, :, pl.ds(pl.multiple_of(at * LANES, LANES), LANES)]

    for rank in range(GROUP):
        layer = layer_ref[group + rank]
        kind = kind_ref[group + rank]
        first = pick(kind, TILE0 + [0])
        offset = rank * WIDE if rank < wide_ranks else wide_ranks * (WIDE - 1) + rank
        is_wide = (kind >= FIRST_WIDE) & (kind < NONE)

        def put(at, value):
            out_ref[0, :, (offset + at) * LANES : (offset + at + 1) * LANES] = value

        def narrow():
            at = first + part
            low = pick(kind, STARTS + [0])
            high = low + pick(kind, WIDTHS + [0])
            column = lane + at * LANES
            keep = (column >= low) & (column < high)
            put(0, jnp.where(keep, tile_of(layer, at).astype(jnp.float32), 0.0).astype(jnp.bfloat16))

        if rank >= wide_ranks:
            narrow()
            continue

        @pl.when(is_wide)
        def _():
            for at in range(WIDE):
                tile = part * WIDE + at
                last = TILES[FIRST_WIDE] - 1
                if at < WIDE - (GROUP * WIDE - TILES[FIRST_WIDE]):
                    put(at, tile_of(layer, first + tile))
                else:
                    value = tile_of(layer, first + jnp.minimum(tile, last)).astype(jnp.float32)
                    put(at, (value * (tile <= last).astype(jnp.float32)).astype(jnp.bfloat16))

        @pl.when(jnp.logical_not(is_wide))
        def _():
            narrow()
            for at in range(1, WIDE):
                put(at, blank)


def build_send(wide_ranks, plan, grads):
    layers, rows, _ = grads.shape
    chips = plan[0].shape[0]
    cols = slot_tiles(wide_ranks) * LANES
    return pl.pallas_call(
        functools.partial(send_kernel, wide_ranks),
        out_shape=jax.ShapeDtypeStruct((chips, rows, cols), jnp.bfloat16),
        grid_spec=pltpu.PrefetchScalarGridSpec(
            num_scalar_prefetch=2,
            grid=(chips,),
            in_specs=[pl.BlockSpec((layers, rows, HALF), lambda i, *_: (0, 0, 0))],
            out_specs=pl.BlockSpec((1, rows, cols), lambda i, *_: (i, 0, 0)),
        ),
        name="build_send",
    )(plan[0], plan[1], grads)


def apply_kernel(wide_ranks, step_ref, core_ref, mine_ref, other_ref, grad_ref, out_ref, sum_ref):
    rank = pl.program_id(0)
    half = mine_ref.shape[1]
    core = core_ref[0]

    def run(tile, tiles):
        columns = pl.ds(pl.multiple_of(tile * LANES, LANES), tiles * LANES)
        block = grad_ref[:, columns]
        total = jnp.float32(0.0)
        for root_ref, side in ((mine_ref, core), (other_ref, 1 - core)):
            value = jnp.dot(root_ref[0], block, preferred_element_type=jnp.float32)
            value = value.astype(jnp.bfloat16)
            out_ref[pl.ds(pl.multiple_of(side * half, half), half), columns] = value
            wide_value = value.astype(jnp.float32)
            total = total + jnp.sum(wide_value * wide_value)
        sum_ref[rank] = total

    @pl.when(rank < wide_ranks)
    def _():
        run(rank * WIDE, WIDE)

    @pl.when(rank >= wide_ranks)
    def _():
        run(wide_ranks * (WIDE - 1) + rank, 1)


def apply_roots(wide_ranks, steps, core, mine, other, gathered):
    half, model_rows = mine.shape[1:]
    cols = gathered.shape[1]
    root_spec = pl.BlockSpec((1, half, model_rows), lambda r, steps, core: (steps[r], 0, 0))
    whole = pl.BlockSpec((model_rows, cols), lambda r, *_: (0, 0))
    return pl.pallas_call(
        functools.partial(apply_kernel, wide_ranks),
        out_shape=[
            jax.ShapeDtypeStruct((model_rows, cols), jnp.bfloat16),
            jax.ShapeDtypeStruct((GROUP,), jnp.float32),
        ],
        grid_spec=pltpu.PrefetchScalarGridSpec(
            num_scalar_prefetch=2,
            grid=(GROUP,),
            in_specs=[root_spec, root_spec, whole],
            out_specs=[whole, pl.BlockSpec(memory_space=pltpu.SMEM)],
        ),
        name="apply_roots",
    )(steps, core, mine, other, gathered)


def gram_kernel(wide_ranks, place_ref, core_ref, mine_ref, other_ref, out_ref):
    rank = pl.program_id(0)
    half = out_ref.shape[1]
    core = core_ref[0]

    def run(tile, tiles):
        columns = pl.ds(pl.multiple_of(tile * LANES, LANES), tiles * LANES)
        rows = pl.ds(pl.multiple_of(core * half, half), half)
        total = None
        for grad_ref in (mine_ref, other_ref):
            term = lax.dot_general(
                grad_ref[rows, columns],
                grad_ref[:, columns],
                (((1,), (1,)), ((), ())),
                preferred_element_type=jnp.float32,
            )
            total = term if total is None else total + term
        out_ref[0] = total.astype(jnp.bfloat16)

    @pl.when(rank < wide_ranks)
    def _():
        run(rank * WIDE, WIDE)

    @pl.when(rank >= wide_ranks)
    def _():
        run(wide_ranks * (WIDE - 1) + rank, 1)


def part_grams(wide_ranks, places, core, mine, other):
    model_rows, cols = mine.shape
    half = model_rows // 2
    whole = pl.BlockSpec((model_rows, cols), lambda r, *_: (0, 0))
    return pl.pallas_call(
        functools.partial(gram_kernel, wide_ranks),
        out_shape=jax.ShapeDtypeStruct((GROUP, half, model_rows), jnp.bfloat16),
        grid_spec=pltpu.PrefetchScalarGridSpec(
            num_scalar_prefetch=2,
            grid=(GROUP,),
            in_specs=[whole, whole],
            out_specs=pl.BlockSpec(
                (1, half, model_rows), lambda r, places, core: (places[r], 0, 0)
            ),
        ),
        name="part_grams",
    )(places, core, mine, other)


def update_kernel(wide_ranks, base_ref, rank_ref, scale_ref, weight_ref, back_ref, out_ref):
    layer = pl.program_id(0)
    rows = back_ref.shape[1]
    lane = lax.broadcasted_iota(jnp.int32, (rows, LANES), 1)
    for tile in range(ALL_TILES):
        step = None
        for kind in range(7):
            at = tile - TILE0[kind]
            if not 0 <= at < TILES[kind]:
                continue
            matrix = layer * 7 + kind
            rank = rank_ref[matrix]
            if kind >= FIRST_WIDE:
                source, column = at // WIDE, rank * WIDE + at % WIDE
            else:
                source, column = at, rank_tile(rank, wide_ranks)
            piece = back_ref[
                base_ref[matrix] + source, :, pl.ds(pl.multiple_of(column * LANES, LANES), LANES)
            ]
            piece = 0.02 * (scale_ref[matrix] * piece.astype(jnp.float32))
            low = STARTS[kind] - tile * LANES
            step = piece if step is None else jnp.where(lane >= low, piece, step)
        where = pl.ds(tile, rows, stride=ALL_TILES)
        out_ref[0, where, :] = weight_ref[0, where, :] - step


def update_weights(wide_ranks, plan, ratio, weights, returned):
    layers, rows = weights.shape[:2]
    view = (layers, rows * ALL_TILES, LANES)
    flat_spec = pl.BlockSpec((1,) + view[1:], lambda l, *_: (l, 0, 0))
    out = pl.pallas_call(
        functools.partial(update_kernel, wide_ranks),
        out_shape=jax.ShapeDtypeStruct(view, jnp.float32),
        grid_spec=pltpu.PrefetchScalarGridSpec(
            num_scalar_prefetch=3,
            grid=(layers,),
            in_specs=[flat_spec, pl.BlockSpec(returned.shape, lambda l, *_: (0, 0, 0))],
            out_specs=flat_spec,
        ),
        name="update_weights",
    )(plan[3], plan[4], ratio.reshape(-1), weights.reshape(view), returned)
    return out.reshape(weights.shape)


def kind_sums(values):
    return jnp.stack(
        [
            jnp.sum(values[:, :, start : start + wide], axis=(1, 2))
            for start, wide in zip(STARTS, WIDTHS)
        ],
        axis=1,
    )


def swap_cores(value):
    return lax.ppermute(value, "tp", [(0, 1), (1, 0)])


def swap_chips(value, step):
    chips = lax.axis_size("fsdp")
    return lax.ppermute(value, "fsdp", [(i, i ^ step) for i in range(chips)])


def sum_everywhere(value):
    value = value + swap_cores(value)
    step = 1
    while step < lax.axis_size("fsdp"):
        value = value + swap_chips(value, step)
        step = 2 * step
    return value


def refresh(
    wide_ranks, plan, grads, weights, adam_m, adam_v, stats, roots, vec_weight, vec_grad, vec_m, vec_v
):
    chips = lax.axis_size("fsdp")
    chip = lax.axis_index("fsdp")
    core = lax.axis_index("tp").astype(jnp.int32)
    layers = grads.shape[0]
    rows = grads.shape[1]
    model_rows = rows * chips
    cols = slot_tiles(wide_ranks) * LANES
    group_first = chip - chip % GROUP
    kinds = lax.dynamic_slice(plan[1], (group_first,), (GROUP,))
    places = lax.dynamic_slice(plan[2], (group_first,), (GROUP,))
    own_part = (chip % GROUP).astype(jnp.int32)
    owned = jnp.any((places == own_part) & (kinds < NONE))
    core_arg = core.reshape(1)

    outgoing = build_send(wide_ranks, plan, grads[:, :, 0, :])
    arrived = lax.all_to_all(outgoing, "fsdp", split_axis=0, concat_axis=0, tiled=True)
    gathered = arrived.reshape(model_rows, cols)

    root_mine = jnp.stack([roots[0]] + [swap_chips(roots[0], step) for step in range(1, GROUP)])
    root_other = swap_cores(root_mine)

    grad_float = grads.astype(jnp.float32)
    adam_m_new = 0.9 * adam_m + 0.1 * grad_float
    adam_v_new = 0.99 * adam_v + 0.01 * grad_float * grad_float
    adam_step = (adam_m_new / (jnp.sqrt(adam_v_new) + 1e-08))[:, :, 0, :]
    adam_part = kind_sums(adam_step * adam_step)

    precond, sums = apply_roots(
        wide_ranks, places ^ own_part, core_arg, root_mine, root_other, gathered
    )
    returned = lax.all_to_all(
        precond.reshape(chips, rows, cols), "fsdp", split_axis=0, concat_axis=0, tiled=True
    )
    ranks = jnp.arange(GROUP, dtype=jnp.int32)
    is_here = (plan[3] == group_first)[:, None] & (plan[4][:, None] == ranks[None, :])
    shampoo_part = jnp.sum(jnp.where(is_here, sums[None, :], 0.0), axis=1).reshape(layers, 7)
    totals = sum_everywhere(jnp.stack([adam_part, shampoo_part]))
    ratio = jnp.sqrt(totals[0]) / (jnp.sqrt(totals[1]) + 1e-06)

    grams = part_grams(wide_ranks, places, core_arg, gathered, swap_cores(gathered))
    groups = [[first + i for i in range(GROUP)] for first in range(0, chips, GROUP)]
    terms = lax.all_to_all(
        grams, "fsdp", split_axis=0, concat_axis=0, tiled=True, axis_index_groups=groups
    )
    stat_term = jnp.sum(terms.astype(jnp.float32), axis=0)
    stats_new = jnp.where(owned, 0.9 * stats[0] + 0.1 * stat_term, stats[0])[None]

    weights_new = update_weights(wide_ranks, plan, ratio, weights, returned)

    vec_float = vec_grad.astype(jnp.float32)
    vec_m_new = 0.9 * vec_m + 0.1 * vec_float
    vec_v_new = 0.99 * vec_v + 0.01 * vec_float * vec_float
    vec_weight_new = vec_weight - 0.02 * vec_m_new / (jnp.sqrt(vec_v_new) + 1e-08)
    return (weights_new, adam_m_new, adam_v_new, stats_new, vec_weight_new, vec_m_new, vec_v_new)


def on_device(owner, *arrays):
    plan = make_plan(owner, lax.axis_size("fsdp"))
    branches = [functools.partial(refresh, wide_ranks) for wide_ranks in range(2, GROUP + 1)]
    return lax.switch(plan[5][0] - 2, branches, plan, *arrays)


def solution(mesh):
    matrix = P(None, "fsdp", "tp", None)
    slot = P("fsdp", "tp", None)
    vector = P(None, ("fsdp", "tp"))
    return jax.shard_map(
        on_device,
        mesh=mesh,
        in_specs=(P(), matrix, matrix, matrix, matrix, slot, slot, vector, vector, vector, vector),
        out_specs=(matrix, matrix, matrix, slot, vector, vector, vector),
        check_vma=False,
    )
```

```python
import functools

import jax
import jax.numpy as jnp
from jax import lax
from jax.experimental import pallas as pl
from jax.experimental.pallas import tpu as pltpu
from jax.sharding import PartitionSpec as P

FF = 4864
QW = 896
KW = 128
LANES = 128
WIDTHS = [QW // 2, KW // 2, KW // 2, QW // 2, FF // 2, FF // 2, FF // 2]
STARTS = [sum(WIDTHS[:kind]) for kind in range(7)]
TILE0 = [start // LANES for start in STARTS]
TILES = [-(-(start + wide) // LANES) - start // LANES for start, wide in zip(STARTS, WIDTHS)]
HALF = sum(WIDTHS)
ALL_TILES = HALF // LANES
GROUP = 4
WIDE = -(-max(TILES) // GROUP)
FIRST_WIDE = 4
NONE = 7


def pick(index, values):
    result = jnp.int32(values[-1])
    for at in range(len(values) - 1):
        result = jnp.where(index == at, values[at], result)
    return result


def row_block(rows):
    return 8 if rows % 8 == 0 else rows


def rank_tile(rank, wide_ranks):
    return jnp.where(rank < wide_ranks, rank * WIDE, wide_ranks * (WIDE - 1) + rank)


def slot_tiles(wide_ranks):
    return wide_ranks * WIDE + GROUP - wide_ranks


def plan_kernel(owner_ref, layer_ref, kind_ref, place_ref, base_ref, rank_ref, level_ref, mat_ref):
    layers = owner_ref.shape[0]
    chips = layer_ref.shape[0]

    def clear(chip, carry):
        mat_ref[chip] = -1
        return carry

    lax.fori_loop(0, chips, clear, 0)

    def name(matrix, carry):
        mat_ref[owner_ref[matrix // 7, matrix % 7]] = matrix
        return carry

    lax.fori_loop(0, layers * 7, name, 0)

    def rank_group(group, level):
        first = group * GROUP
        mats = [mat_ref[first + i] for i in range(GROUP)]
        wide = [((m >= 0) & (m % 7 >= FIRST_WIDE)).astype(jnp.int32) for m in mats]
        count = sum(wide)
        before_wide = jnp.int32(0)
        before_rest = count
        for i in range(GROUP):
            rank = jnp.where(wide[i] == 1, before_wide, before_rest)
            before_wide = before_wide + wide[i]
            before_rest = before_rest + 1 - wide[i]
            there = first + rank
            layer_ref[there] = jnp.maximum(mats[i], 0) // 7
            kind_ref[there] = jnp.where(mats[i] >= 0, jnp.maximum(mats[i], 0) % 7, NONE)
            place_ref[there] = i

            @pl.when(mats[i] >= 0)
            def _():
                base_ref[mats[i]] = first
                rank_ref[mats[i]] = rank

        return jnp.maximum(level, count)

    level_ref[0] = lax.fori_loop(0, chips // GROUP, rank_group, jnp.int32(0))


def make_plan(owner, chips):
    matrices = owner.shape[0] * 7
    sizes = [chips, chips, chips, matrices, matrices, 1]
    smem = pl.BlockSpec(memory_space=pltpu.SMEM)
    return pl.pallas_call(
        plan_kernel,
        out_shape=[jax.ShapeDtypeStruct((size,), jnp.int32) for size in sizes],
        in_specs=[smem],
        out_specs=[smem] * len(sizes),
        scratch_shapes=[pltpu.SMEM((chips,), jnp.int32)],
        name="plan",
    )(owner)


def send_kernel(wide_ranks, layer_ref, kind_ref, grad_ref, out_ref):
    group = pl.program_id(0) * GROUP
    rows = grad_ref.shape[1]
    lane = lax.broadcasted_iota(jnp.int32, (rows, LANES), 1)
    last = max(TILES) - 1

    def tile_of(layer, at):
        return grad_ref[layer, :, pl.ds(pl.multiple_of(at * LANES, LANES), LANES)]

    def fill(part, carry):
        for rank in range(GROUP):
            layer = layer_ref[group + rank]
            kind = kind_ref[group + rank]
            first = pick(kind, TILE0 + [0])
            offset = rank * WIDE if rank < wide_ranks else wide_ranks * (WIDE - 1) + rank

            def put(at, value):
                out_ref[part, :, (offset + at) * LANES : (offset + at + 1) * LANES] = value

            def narrow():
                at = first + part
                low = pick(kind, STARTS + [0])
                high = low + pick(kind, WIDTHS + [0])
                column = lane + at * LANES
                value = jnp.where(
                    (column >= low) & (column < high), tile_of(layer, at).astype(jnp.float32), 0.0
                )
                put(0, value.astype(jnp.bfloat16))

            if rank >= wide_ranks:
                narrow()
                continue

            is_wide = (kind >= FIRST_WIDE) & (kind < NONE)

            @pl.when(is_wide)
            def _():
                for at in range(WIDE):
                    tile = part * WIDE + at
                    value = tile_of(layer, first + jnp.minimum(tile, last))
                    if (GROUP - 1) * WIDE + at > last:
                        value = value.astype(jnp.float32) * (tile <= last).astype(jnp.float32)
                    put(at, value.astype(jnp.bfloat16))

            @pl.when(jnp.logical_not(is_wide))
            def _():
                narrow()
                for at in range(1, WIDE):
                    put(at, jnp.zeros((rows, LANES), jnp.bfloat16))

        return carry

    lax.fori_loop(0, GROUP, fill, 0)


def build_send(wide_ranks, plan, grads):
    layers, rows, _ = grads.shape
    chips = plan[0].shape[0]
    cols = slot_tiles(wide_ranks) * LANES
    return pl.pallas_call(
        functools.partial(send_kernel, wide_ranks),
        out_shape=jax.ShapeDtypeStruct((chips, rows, cols), jnp.bfloat16),
        grid_spec=pltpu.PrefetchScalarGridSpec(
            num_scalar_prefetch=2,
            grid=(chips // GROUP,),
            in_specs=[pl.BlockSpec((layers, rows, HALF), lambda g, *_: (0, 0, 0))],
            out_specs=pl.BlockSpec((GROUP, rows, cols), lambda g, *_: (g, 0, 0)),
        ),
        name="build_send",
    )(plan[0], plan[1], grads)


def adam_kernel(grad_ref, m_ref, v_ref, m_out, v_out, sum_ref, grad_flat, total_ref):
    layer = pl.program_id(0)
    block = grad_ref.shape[1]
    for tile in range(ALL_TILES):
        piece = grad_ref[0, :, tile * LANES : (tile + 1) * LANES]
        grad_flat[pl.ds(tile, block, stride=ALL_TILES), :] = piece.astype(jnp.float32)
    grad = grad_flat[...]
    m_new = 0.9 * m_ref[0] + 0.1 * grad
    v_new = 0.99 * v_ref[0] + 0.01 * grad * grad
    m_out[0] = m_new
    v_out[0] = v_new
    step = m_new / (jnp.sqrt(v_new) + 1e-08)
    square = step * step

    @pl.when(pl.program_id(1) == 0)
    def _():
        total_ref[...] = square

    @pl.when(pl.program_id(1) > 0)
    def _():
        total_ref[...] += square

    @pl.when(pl.program_id(1) == pl.num_programs(1) - 1)
    def _():
        by_column = total_ref[0:ALL_TILES, :]
        for row in range(1, block):
            by_column = by_column + total_ref[row * ALL_TILES : (row + 1) * ALL_TILES, :]
        column = lax.broadcasted_iota(jnp.int32, by_column.shape, 0) * LANES
        column = column + lax.broadcasted_iota(jnp.int32, by_column.shape, 1)
        for kind in range(7):
            keep = (column >= STARTS[kind]) & (column < STARTS[kind] + WIDTHS[kind])
            sum_ref[layer, kind] = jnp.sum(jnp.where(keep, by_column, 0.0))


def adam_update(grads, adam_m, adam_v):
    layers, rows, _ = grads.shape
    block = row_block(rows)
    blocks = rows // block
    view = (layers * blocks, block * ALL_TILES, LANES)
    flat_spec = pl.BlockSpec((1,) + view[1:], lambda l, r: (l * blocks + r, 0, 0))
    flat = jax.ShapeDtypeStruct(view, jnp.float32)
    count = layers * rows * HALF
    m_new, v_new, sums = pl.pallas_call(
        adam_kernel,
        out_shape=[flat, flat, jax.ShapeDtypeStruct((layers, 7), jnp.float32)],
        grid_spec=pltpu.PrefetchScalarGridSpec(
            num_scalar_prefetch=0,
            grid=(layers, blocks),
            in_specs=[pl.BlockSpec((1, block, HALF), lambda l, r: (l, r, 0)), flat_spec, flat_spec],
            out_specs=[flat_spec, flat_spec, pl.BlockSpec(memory_space=pltpu.SMEM)],
            scratch_shapes=[pltpu.VMEM(view[1:], jnp.float32), pltpu.VMEM(view[1:], jnp.float32)],
        ),
        cost_estimate=pl.CostEstimate(
            flops=12 * count, bytes_accessed=18 * count, transcendentals=2 * count
        ),
        name="adam_update",
    )(grads, adam_m.reshape(view), adam_v.reshape(view))
    return m_new.reshape(adam_m.shape), v_new.reshape(adam_v.shape), sums


def apply_kernel(wide_ranks, step_ref, core_ref, *refs):
    root_refs = refs[: 2 * GROUP]
    grad_hbm, out_hbm, sum_ref, root_buf, grad_buf, out_buf, root_sem, grad_sem, out_sem = refs[
        2 * GROUP :
    ]
    half = root_refs[0].shape[0]
    core = core_ref[0]

    def columns(rank):
        if rank < wide_ranks:
            return pl.ds(rank * WIDE * LANES, WIDE * LANES)
        return pl.ds((wide_ranks * (WIDE - 1) + rank) * LANES, LANES)

    def root_copy(step, rank, side):
        at = pl.multiple_of((core if side == 0 else 1 - core) * half, half)
        return pltpu.make_async_copy(
            root_refs[2 * step + side],
            root_buf.at[rank, pl.ds(at, half), :],
            root_sem.at[rank, side],
        )

    def grad_copy(rank):
        part = columns(rank)
        return pltpu.make_async_copy(
            grad_hbm.at[:, part], grad_buf.at[:, part], grad_sem.at[rank]
        )

    def out_copy(rank):
        part = columns(rank)
        return pltpu.make_async_copy(out_buf.at[:, part], out_hbm.at[:, part], out_sem.at[rank])

    for rank in range(GROUP):
        grad_copy(rank).start()
        for step in range(GROUP):

            @pl.when(step_ref[rank] == step)
            def _():
                root_copy(step, rank, 0).start()
                root_copy(step, rank, 1).start()

    def run(rank, tile, tiles):
        part = pl.ds(pl.multiple_of(tile * LANES, LANES), tiles * LANES)
        value = jnp.dot(root_buf[rank], grad_buf[:, part], preferred_element_type=jnp.float32)
        value = value.astype(jnp.bfloat16)
        out_buf[:, part] = value
        value = value.astype(jnp.float32)
        sum_ref[rank] = jnp.sum(value * value)

    for rank in range(GROUP):
        grad_copy(rank).wait()
        root_copy(0, rank, 0).wait()
        root_copy(0, rank, 1).wait()
        if rank < wide_ranks:
            run(rank, rank * WIDE, WIDE)
        else:
            run(rank, wide_ranks * (WIDE - 1) + rank, 1)
        out_copy(rank).start()
    for rank in range(GROUP):
        out_copy(rank).wait()


def apply_roots(wide_ranks, steps, core, roots, gathered):
    half, model_rows = roots[0].shape
    cols = gathered.shape[1]
    anywhere = pl.BlockSpec(memory_space=pl.ANY)
    return pl.pallas_call(
        functools.partial(apply_kernel, wide_ranks),
        out_shape=[
            jax.ShapeDtypeStruct((model_rows, cols), jnp.bfloat16),
            jax.ShapeDtypeStruct((GROUP,), jnp.float32),
        ],
        grid_spec=pltpu.PrefetchScalarGridSpec(
            num_scalar_prefetch=2,
            grid=(1,),
            in_specs=[anywhere] * (2 * GROUP + 1),
            out_specs=[anywhere, pl.BlockSpec(memory_space=pltpu.SMEM)],
            scratch_shapes=[
                pltpu.VMEM((GROUP, model_rows, model_rows), jnp.bfloat16),
                pltpu.VMEM((model_rows, cols), jnp.bfloat16),
                pltpu.VMEM((model_rows, cols), jnp.bfloat16),
                pltpu.SemaphoreType.DMA((GROUP, 2)),
                pltpu.SemaphoreType.DMA((GROUP,)),
                pltpu.SemaphoreType.DMA((GROUP,)),
            ],
        ),
        name="apply_roots",
    )(steps, core, *roots, gathered)


def gram_kernel(wide_ranks, step_ref, core_ref, mine_ref, other_ref, *refs):
    out_refs = refs[:GROUP]
    out_buf, out_sem = refs[GROUP:]
    rank = pl.program_id(0)
    half = out_buf.shape[1]
    core = core_ref[0]

    def run(tile, tiles):
        columns = pl.ds(pl.multiple_of(tile * LANES, LANES), tiles * LANES)
        rows = pl.ds(pl.multiple_of(core * half, half), half)
        total = None
        for grad_ref in (mine_ref, other_ref):
            term = lax.dot_general(
                grad_ref[rows, columns],
                grad_ref[:, columns],
                (((1,), (1,)), ((), ())),
                preferred_element_type=jnp.float32,
            )
            total = term if total is None else total + term
        out_buf[rank] = total.astype(jnp.bfloat16)

    @pl.when(rank < wide_ranks)
    def _():
        run(rank * WIDE, WIDE)

    @pl.when(rank >= wide_ranks)
    def _():
        run(wide_ranks * (WIDE - 1) + rank, 1)

    def out_copy(step, at):
        return pltpu.make_async_copy(out_buf.at[at], out_refs[step], out_sem.at[at])

    for step in range(GROUP):

        @pl.when(step_ref[rank] == step)
        def _():
            out_copy(step, rank).start()

    @pl.when(rank == GROUP - 1)
    def _():
        for at in range(GROUP):
            out_copy(0, at).wait()


def part_grams(wide_ranks, steps, core, mine, other):
    model_rows, cols = mine.shape
    half = model_rows // 2
    whole = pl.BlockSpec((model_rows, cols), lambda r, *_: (0, 0))
    return pl.pallas_call(
        functools.partial(gram_kernel, wide_ranks),
        out_shape=[jax.ShapeDtypeStruct((half, model_rows), jnp.bfloat16)] * GROUP,
        grid_spec=pltpu.PrefetchScalarGridSpec(
            num_scalar_prefetch=2,
            grid=(GROUP,),
            in_specs=[whole, whole],
            out_specs=[pl.BlockSpec(memory_space=pl.ANY)] * GROUP,
            scratch_shapes=[
                pltpu.VMEM((GROUP, half, model_rows), jnp.bfloat16),
                pltpu.SemaphoreType.DMA((GROUP,)),
            ],
        ),
        name="part_grams",
    )(steps, core, mine, other)


def update_kernel(
    wide_ranks, base_ref, rank_ref, scale_ref, weight_ref, back_ref, out_ref, done_ref
):
    layer = pl.program_id(0)
    done_ref[0] = layer
    rows = back_ref.shape[1]
    lane = lax.broadcasted_iota(jnp.int32, (rows, LANES), 1)
    for tile in range(ALL_TILES):
        step = None
        for kind in range(7):
            at = tile - TILE0[kind]
            if not 0 <= at < TILES[kind]:
                continue
            matrix = layer * 7 + kind
            rank = rank_ref[matrix]
            if kind >= FIRST_WIDE:
                source, column = at // WIDE, rank * WIDE + at % WIDE
            else:
                source, column = at, rank_tile(rank, wide_ranks)
            piece = back_ref[
                base_ref[matrix] + source, :, pl.ds(pl.multiple_of(column * LANES, LANES), LANES)
            ]
            piece = 0.02 * (scale_ref[matrix] * piece.astype(jnp.float32))
            low = STARTS[kind] - tile * LANES
            step = piece if step is None else jnp.where(lane >= low, piece, step)
        where = pl.ds(tile, rows, stride=ALL_TILES)
        out_ref[0, where, :] = weight_ref[0, where, :] - step


def update_weights(wide_ranks, plan, ratio, weights, returned):
    layers, rows = weights.shape[:2]
    view = (layers, rows * ALL_TILES, LANES)
    flat_spec = pl.BlockSpec((1,) + view[1:], lambda l, *_: (l, 0, 0))
    out, done = pl.pallas_call(
        functools.partial(update_kernel, wide_ranks),
        out_shape=[
            jax.ShapeDtypeStruct(view, jnp.float32),
            jax.ShapeDtypeStruct((1,), jnp.int32),
        ],
        grid_spec=pltpu.PrefetchScalarGridSpec(
            num_scalar_prefetch=3,
            grid=(layers,),
            in_specs=[flat_spec, pl.BlockSpec(returned.shape, lambda l, *_: (0, 0, 0))],
            out_specs=[flat_spec, pl.BlockSpec(memory_space=pltpu.SMEM)],
        ),
        name="update_weights",
    )(plan[3], plan[4], ratio.reshape(-1), weights.reshape(view), returned)
    return out.reshape(weights.shape), done


def swap_cores(value):
    return lax.ppermute(value, "tp", [(0, 1), (1, 0)])


def swap_chips(value, step):
    chips = lax.axis_size("fsdp")
    return lax.ppermute(value, "fsdp", [(i, i ^ step) for i in range(chips)])


def sum_over(value, step):
    return value + sum(swap_chips(value, step * other) for other in range(1, 4))


def refresh(
    wide_ranks, plan, grads, weights, adam_m, adam_v, stats, roots, vec_weight, vec_grad, vec_m, vec_v
):
    chips = lax.axis_size("fsdp")
    chip = lax.axis_index("fsdp")
    core = lax.axis_index("tp").astype(jnp.int32)
    layers = grads.shape[0]
    rows = grads.shape[1]
    model_rows = rows * chips
    cols = slot_tiles(wide_ranks) * LANES
    group_first = chip - chip % GROUP
    kinds = lax.dynamic_slice(plan[1], (group_first,), (GROUP,))
    places = lax.dynamic_slice(plan[2], (group_first,), (GROUP,))
    own_part = (chip % GROUP).astype(jnp.int32)
    owned = jnp.any((places == own_part) & (kinds < NONE))
    core_arg = core.reshape(1)
    steps = places ^ own_part

    outgoing = build_send(wide_ranks, plan, grads[:, :, 0, :])
    arrived = lax.all_to_all(outgoing, "fsdp", split_axis=0, concat_axis=0, tiled=True)
    adam_m_new, adam_v_new, adam_part = adam_update(grads[:, :, 0, :], adam_m, adam_v)
    along_x = swap_chips(roots[0], 1)
    along_y = swap_chips(roots[0], 2)
    along_x, along_y, adam_part = lax.optimization_barrier((along_x, along_y, adam_part))
    forward = jnp.where(core == 0, along_y, along_x)
    across = lax.ppermute(
        forward,
        ("fsdp", "tp"),
        [(2 * i + side, 2 * (i ^ (1 + side)) + side) for i in range(chips) for side in range(2)],
    )
    group_roots = [along_x, along_y, across]
    all_roots = []
    for part in [roots[0]] + group_roots:
        all_roots += [part, swap_cores(part)]

    arrived, all_roots, adam_part = lax.optimization_barrier((arrived, all_roots, adam_part))
    gathered = arrived.reshape(model_rows, cols)
    precond, sums = apply_roots(wide_ranks, steps, core_arg, all_roots, gathered)
    returned = lax.all_to_all(
        precond.reshape(chips, rows, cols), "fsdp", split_axis=0, concat_axis=0, tiled=True
    )
    ranks = jnp.arange(GROUP, dtype=jnp.int32)
    is_here = (plan[3] == group_first)[:, None] & (plan[4][:, None] == ranks[None, :])
    shampoo_part = jnp.sum(jnp.where(is_here, sums[None, :], 0.0), axis=1).reshape(layers, 7)
    totals = jnp.stack([adam_part, shampoo_part])
    totals = totals + swap_cores(totals)
    beside = [totals] + [swap_chips(totals, step) for step in range(1, GROUP)]
    grams = part_grams(wide_ranks, steps, core_arg, gathered, swap_cores(gathered))
    grams, beside = lax.optimization_barrier((grams, beside))
    totals = sum(beside)
    step = GROUP
    while step < chips:
        totals = sum_over(totals, step)
        step = 4 * step
    ratio = jnp.sqrt(totals[0]) / (jnp.sqrt(totals[1]) + 1e-06)
    terms = [grams[0]] + [swap_chips(grams[step], step) for step in range(1, GROUP)]

    weights_new, done = update_weights(wide_ranks, plan, ratio, weights, returned)

    stat_term = sum(term.astype(jnp.float32) for term in terms)
    owned = owned & (done[0] >= 0)
    stats_new = jnp.where(owned, 0.9 * stats[0] + 0.1 * stat_term, stats[0])[None]

    vec_float = vec_grad.astype(jnp.float32)
    vec_m_new = 0.9 * vec_m + 0.1 * vec_float
    vec_v_new = 0.99 * vec_v + 0.01 * vec_float * vec_float
    vec_weight_new = vec_weight - 0.02 * vec_m_new / (jnp.sqrt(vec_v_new) + 1e-08)
    return (weights_new, adam_m_new, adam_v_new, stats_new, vec_weight_new, vec_m_new, vec_v_new)


def on_device(owner, *arrays):
    plan = make_plan(owner, lax.axis_size("fsdp"))
    branches = [functools.partial(refresh, wide_ranks) for wide_ranks in range(2, GROUP + 1)]
    return lax.switch(plan[5][0] - 2, branches, plan, *arrays)


def solution(mesh):
    matrix = P(None, "fsdp", "tp", None)
    slot = P("fsdp", "tp", None)
    vector = P(None, ("fsdp", "tp"))
    return jax.shard_map(
        on_device,
        mesh=mesh,
        in_specs=(P(), matrix, matrix, matrix, matrix, slot, slot, vector, vector, vector, vector),
        out_specs=(matrix, matrix, matrix, slot, vector, vector, vector),
        check_vma=False,
    )
```

```python
import functools

import jax
import jax.numpy as jnp
from jax import lax
from jax.experimental import pallas as pl
from jax.experimental.pallas import tpu as pltpu
from jax.sharding import PartitionSpec as P

FF = 4864
QW = 896
KW = 128
LANES = 128
WIDTHS = [QW // 2, KW // 2, KW // 2, QW // 2, FF // 2, FF // 2, FF // 2]
STARTS = [sum(WIDTHS[:kind]) for kind in range(7)]
TILE0 = [start // LANES for start in STARTS]
TILES = [-(-(start + wide) // LANES) - start // LANES for start, wide in zip(STARTS, WIDTHS)]
HALF = sum(WIDTHS)
ALL_TILES = HALF // LANES
GROUP = 4
WIDE = -(-max(TILES) // GROUP)
FIRST_WIDE = 4
NONE = 7
GROUPINGS = [(0, 1)]


def pick(index, values):
    result = jnp.int32(values[-1])
    for at in range(len(values) - 1):
        result = jnp.where(index == at, values[at], result)
    return result


def bit_order(grouping, chips):
    return list(grouping) + [at for at in range(chips.bit_length() - 1) if at not in grouping]


def chip_at(place, order):
    return sum(((place >> at) & 1) << bit for at, bit in enumerate(order))


def place_of(chip, order):
    return sum(((chip >> bit) & 1) << at for at, bit in enumerate(order))


def row_block(rows):
    return 8 if rows % 8 == 0 else rows


def rank_tile(rank, wide_ranks):
    return jnp.where(rank < wide_ranks, rank * WIDE, wide_ranks * (WIDE - 1) + rank)


def slot_tiles(wide_ranks):
    return wide_ranks * WIDE + GROUP - wide_ranks


def plan_kernel(
    owner_ref, layer_ref, kind_ref, place_ref, base_ref, rank_ref, branch_ref, mat_ref, wide_ref
):
    layers = owner_ref.shape[0]
    chips = layer_ref.shape[0]
    orders = [bit_order(grouping, chips) for grouping in GROUPINGS]

    def clear(chip, carry):
        mat_ref[chip] = -1
        wide_ref[chip] = 0
        return carry

    lax.fori_loop(0, chips, clear, 0)

    def name(matrix, carry):
        layer = matrix // 7
        kind = matrix - layer * 7
        chip = owner_ref[layer, kind]
        mat_ref[chip] = matrix
        wide_ref[chip] = (kind >= FIRST_WIDE).astype(jnp.int32)
        return carry

    lax.fori_loop(0, layers * 7, name, 0)

    most = []
    for order in orders:
        level = jnp.int32(0)
        for first in range(0, chips, GROUP):
            count = sum(wide_ref[chip_at(first + i, order)] for i in range(GROUP))
            level = jnp.maximum(level, count)
        most.append(level)
    chosen = jnp.int32(len(orders))
    for at in reversed(range(len(orders))):
        chosen = jnp.where(most[at] <= 2, at, chosen)
    branch_ref[0] = jnp.where(chosen < len(orders), chosen, len(orders) - 3 + most[0])
    order = [pick(chosen, [one[at] for one in orders + orders[:1]]) for at in range(len(orders[0]))]

    def rank_group(group, carry):
        first = group * GROUP
        base = chip_at(first, order)
        members = [base + ((i & 1) << order[0]) + ((i >> 1) << order[1]) for i in range(GROUP)]
        wide = [wide_ref[member] for member in members]
        before_wide = jnp.int32(0)
        before_rest = sum(wide)
        for i in range(GROUP):
            matrix = mat_ref[members[i]]
            rank = jnp.where(wide[i] == 1, before_wide, before_rest)
            before_wide = before_wide + wide[i]
            before_rest = before_rest + 1 - wide[i]
            there = first + rank
            layer = jnp.maximum(matrix, 0) // 7
            layer_ref[there] = layer
            kind_ref[there] = jnp.where(matrix >= 0, matrix - layer * 7, NONE)
            place_ref[there] = i

            @pl.when(matrix >= 0)
            def _():
                base_ref[matrix] = base
                rank_ref[matrix] = rank

        return carry

    lax.fori_loop(0, chips // GROUP, rank_group, 0)


def make_plan(owner, chips):
    matrices = owner.shape[0] * 7
    sizes = [chips, chips, chips, matrices, matrices, 1]
    smem = pl.BlockSpec(memory_space=pltpu.SMEM)
    return pl.pallas_call(
        plan_kernel,
        out_shape=[jax.ShapeDtypeStruct((size,), jnp.int32) for size in sizes],
        in_specs=[smem],
        out_specs=[smem] * len(sizes),
        scratch_shapes=[pltpu.SMEM((chips,), jnp.int32)] * 2,
        name="plan",
    )(owner)


def send_kernel(wide_ranks, order, layer_ref, kind_ref, grad_ref, out_hbm, out_ref, out_sem):
    group = pl.program_id(0) * GROUP
    chips = out_ref.shape[0]
    rows = grad_ref.shape[1]
    lane = lax.broadcasted_iota(jnp.int32, (rows, LANES), 1)
    last = max(TILES) - 1

    def tile_of(layer, at):
        return grad_ref[layer, :, pl.ds(pl.multiple_of(at * LANES, LANES), LANES)]

    def fill(part, carry):
        for rank in range(GROUP):
            layer = layer_ref[group + rank]
            kind = kind_ref[group + rank]
            first = pick(kind, TILE0 + [0])
            offset = rank * WIDE if rank < wide_ranks else wide_ranks * (WIDE - 1) + rank

            def put(at, value):
                out_ref[group + part, :, (offset + at) * LANES : (offset + at + 1) * LANES] = value

            def narrow():
                at = first + part
                low = pick(kind, STARTS + [0])
                high = low + pick(kind, WIDTHS + [0])
                column = lane + at * LANES
                value = jnp.where(
                    (column >= low) & (column < high), tile_of(layer, at).astype(jnp.float32), 0.0
                )
                put(0, value.astype(jnp.bfloat16))

            if rank >= wide_ranks:
                narrow()
                continue

            is_wide = (kind >= FIRST_WIDE) & (kind < NONE)

            @pl.when(is_wide)
            def _():
                for at in range(WIDE):
                    tile = part * WIDE + at
                    value = tile_of(layer, first + jnp.minimum(tile, last))
                    if (GROUP - 1) * WIDE + at > last:
                        value = value.astype(jnp.float32) * (tile <= last).astype(jnp.float32)
                    put(at, value.astype(jnp.bfloat16))

            @pl.when(jnp.logical_not(is_wide))
            def _():
                narrow()
                for at in range(1, WIDE):
                    put(at, jnp.zeros((rows, LANES), jnp.bfloat16))

        out_copy(group + part).start()
        return carry

    def out_copy(place):
        return pltpu.make_async_copy(
            out_ref.at[place], out_hbm.at[chip_at(place, order)], out_sem.at[place]
        )

    def wait(place, carry):
        out_copy(place).wait()
        return carry

    lax.fori_loop(0, GROUP, fill, 0)

    @pl.when(pl.program_id(0) == pl.num_programs(0) - 1)
    def _():
        lax.fori_loop(0, chips, wait, 0)


def build_send(wide_ranks, order, plan, grads):
    layers, rows, _ = grads.shape
    chips = plan[0].shape[0]
    cols = slot_tiles(wide_ranks) * LANES
    return pl.pallas_call(
        functools.partial(send_kernel, wide_ranks, order),
        out_shape=jax.ShapeDtypeStruct((chips, rows, cols), jnp.bfloat16),
        grid_spec=pltpu.PrefetchScalarGridSpec(
            num_scalar_prefetch=2,
            grid=(chips // GROUP,),
            in_specs=[pl.BlockSpec((layers, rows, HALF), lambda g, *_: (0, 0, 0))],
            out_specs=pl.BlockSpec(memory_space=pl.ANY),
            scratch_shapes=[
                pltpu.VMEM((chips, rows, cols), jnp.bfloat16),
                pltpu.SemaphoreType.DMA((chips,)),
            ],
        ),
        name="build_send",
    )(plan[0], plan[1], grads)


def adam_kernel(grad_ref, m_ref, v_ref, m_out, v_out, sum_ref, grad_flat, total_ref):
    layer = pl.program_id(0)
    block = grad_ref.shape[1]
    for tile in range(ALL_TILES):
        piece = grad_ref[0, :, tile * LANES : (tile + 1) * LANES]
        grad_flat[pl.ds(tile, block, stride=ALL_TILES), :] = piece.astype(jnp.float32)
    grad = grad_flat[...]
    m_new = 0.9 * m_ref[0] + 0.1 * grad
    v_new = 0.99 * v_ref[0] + 0.01 * grad * grad
    m_out[0] = m_new
    v_out[0] = v_new
    step = m_new / (jnp.sqrt(v_new) + 1e-08)
    square = step * step

    @pl.when(pl.program_id(1) == 0)
    def _():
        total_ref[...] = square

    @pl.when(pl.program_id(1) > 0)
    def _():
        total_ref[...] += square

    @pl.when(pl.program_id(1) == pl.num_programs(1) - 1)
    def _():
        by_column = total_ref[0:ALL_TILES, :]
        for row in range(1, block):
            by_column = by_column + total_ref[row * ALL_TILES : (row + 1) * ALL_TILES, :]
        column = lax.broadcasted_iota(jnp.int32, by_column.shape, 0) * LANES
        column = column + lax.broadcasted_iota(jnp.int32, by_column.shape, 1)
        for kind in range(7):
            keep = (column >= STARTS[kind]) & (column < STARTS[kind] + WIDTHS[kind])
            sum_ref[layer, kind] = jnp.sum(jnp.where(keep, by_column, 0.0))


def adam_update(grads, adam_m, adam_v):
    layers, rows, _ = grads.shape
    block = row_block(rows)
    blocks = rows // block
    view = (layers * blocks, block * ALL_TILES, LANES)
    flat_spec = pl.BlockSpec((1,) + view[1:], lambda l, r: (l * blocks + r, 0, 0))
    flat = jax.ShapeDtypeStruct(view, jnp.float32)
    count = layers * rows * HALF
    m_new, v_new, sums = pl.pallas_call(
        adam_kernel,
        out_shape=[flat, flat, jax.ShapeDtypeStruct((layers, 7), jnp.float32)],
        grid_spec=pltpu.PrefetchScalarGridSpec(
            num_scalar_prefetch=0,
            grid=(layers, blocks),
            in_specs=[pl.BlockSpec((1, block, HALF), lambda l, r: (l, r, 0)), flat_spec, flat_spec],
            out_specs=[flat_spec, flat_spec, pl.BlockSpec(memory_space=pltpu.SMEM)],
            scratch_shapes=[pltpu.VMEM(view[1:], jnp.float32), pltpu.VMEM(view[1:], jnp.float32)],
        ),
        cost_estimate=pl.CostEstimate(
            flops=12 * count, bytes_accessed=18 * count, transcendentals=2 * count
        ),
        name="adam_update",
    )(grads, adam_m.reshape(view), adam_v.reshape(view))
    return m_new.reshape(adam_m.shape), v_new.reshape(adam_v.shape), sums


def apply_kernel(wide_ranks, step_ref, core_ref, *refs):
    root_refs = refs[: 2 * GROUP]
    grad_hbm, out_hbm, sum_ref, root_buf, grad_buf, out_buf, root_sem, grad_sem, out_sem = refs[
        2 * GROUP :
    ]
    half = root_refs[0].shape[0]
    core = core_ref[0]

    def columns(rank):
        if isinstance(rank, int):
            if rank < wide_ranks:
                return pl.ds(rank * WIDE * LANES, WIDE * LANES)
            return pl.ds((wide_ranks * (WIDE - 1) + rank) * LANES, LANES)
        return pl.ds(pl.multiple_of(rank * WIDE * LANES, LANES), WIDE * LANES)

    def root_copy(step, rank, side):
        at = pl.multiple_of((core if side == 0 else 1 - core) * half, half)
        return pltpu.make_async_copy(
            root_refs[2 * step + side],
            root_buf.at[rank, pl.ds(at, half), :],
            root_sem.at[rank, side],
        )

    def grad_copy_of(rank, part, source, target, sem):
        return pltpu.make_async_copy(source.at[:, part], target.at[:, part], sem.at[rank])

    for rank in range(GROUP):
        grad_copy_of(rank, columns(rank), grad_hbm, grad_buf, grad_sem).start()
        for step in range(GROUP):

            @pl.when(step_ref[rank] == step)
            def _():
                root_copy(step, rank, 0).start()
                root_copy(step, rank, 1).start()

    def run(rank, part):
        grad_copy_of(rank, part, grad_hbm, grad_buf, grad_sem).wait()
        root_copy(0, rank, 0).wait()
        root_copy(0, rank, 1).wait()

        def side(at, total):
            rows = pl.ds(pl.multiple_of(at * half, half), half)
            value = jnp.dot(
                root_buf[rank, rows, :], grad_buf[:, part], preferred_element_type=jnp.float32
            )
            value = value.astype(jnp.bfloat16)
            out_buf[rows, part] = value
            value = value.astype(jnp.float32)
            return total + jnp.sum((value * value).reshape(half // 8, 8, -1), axis=0)

        total = lax.fori_loop(0, 2, side, jnp.zeros((8, part.size), jnp.float32))
        sum_ref[rank] = jnp.sum(total)
        grad_copy_of(rank, part, out_buf, out_hbm, out_sem).start()

    def wide(rank, carry):
        run(rank, columns(rank))
        return carry

    lax.fori_loop(0, wide_ranks, wide, 0)
    for rank in range(wide_ranks, GROUP):
        run(rank, columns(rank))
    for rank in range(GROUP):
        grad_copy_of(rank, columns(rank), out_buf, out_hbm, out_sem).wait()


def apply_roots(wide_ranks, steps, core, roots, gathered):
    half, model_rows = roots[0].shape
    cols = gathered.shape[1]
    anywhere = pl.BlockSpec(memory_space=pl.ANY)
    return pl.pallas_call(
        functools.partial(apply_kernel, wide_ranks),
        out_shape=[
            jax.ShapeDtypeStruct((model_rows, cols), jnp.bfloat16),
            jax.ShapeDtypeStruct((GROUP,), jnp.float32),
        ],
        grid_spec=pltpu.PrefetchScalarGridSpec(
            num_scalar_prefetch=2,
            grid=(1,),
            in_specs=[anywhere] * (2 * GROUP + 1),
            out_specs=[anywhere, pl.BlockSpec(memory_space=pltpu.SMEM)],
            scratch_shapes=[
                pltpu.VMEM((GROUP, model_rows, model_rows), jnp.bfloat16),
                pltpu.VMEM((model_rows, cols), jnp.bfloat16),
                pltpu.VMEM((model_rows, cols), jnp.bfloat16),
                pltpu.SemaphoreType.DMA((GROUP, 2)),
                pltpu.SemaphoreType.DMA((GROUP,)),
                pltpu.SemaphoreType.DMA((GROUP,)),
            ],
        ),
        name="apply_roots",
    )(steps, core, *roots, gathered)


def gram_kernel(wide_ranks, step_ref, core_ref, mine_ref, other_ref, *refs):
    out_refs = refs[:GROUP]
    keep_buf, send_buf, out_sem = refs[GROUP:]
    rank = pl.program_id(0)
    half = keep_buf.shape[1]
    core = core_ref[0]
    step = step_ref[rank]
    near = step == 1 + core
    far = step == 2 - core

    def run(tile, tiles):
        columns = pl.ds(pl.multiple_of(tile * LANES, LANES), tiles * LANES)
        rows = pl.ds(pl.multiple_of(core * half, half), half)
        total = None
        for grad_ref in (mine_ref, other_ref):
            term = lax.dot_general(
                grad_ref[rows, columns],
                grad_ref[:, columns],
                (((1,), (1,)), ((), ())),
                preferred_element_type=jnp.float32,
            )
            total = term if total is None else total + term

        @pl.when((step == 0) | far)
        def _():
            keep_buf[jnp.minimum(step, 1)] = total

        @pl.when(near | (step == 3))
        def _():
            send_buf[jnp.maximum(step, 2) - 2] = total.astype(jnp.bfloat16)

    @pl.when(rank < wide_ranks)
    def _():
        run(rank * WIDE, WIDE)

    @pl.when(rank >= wide_ranks)
    def _():
        run(wide_ranks * (WIDE - 1) + rank, 1)

    def out_copy(at):
        source = keep_buf.at[at] if at < 2 else send_buf.at[at - 2]
        return pltpu.make_async_copy(source, out_refs[at], out_sem.at[at])

    @pl.when(step == 0)
    def _():
        out_copy(0).start()

    @pl.when(far)
    def _():
        out_copy(1).start()

    @pl.when(near)
    def _():
        out_copy(2).start()

    @pl.when(step == 3)
    def _():
        out_copy(3).start()

    @pl.when(rank == GROUP - 1)
    def _():
        for at in range(GROUP):
            out_copy(at).wait()


def part_grams(wide_ranks, steps, core, mine, other):
    model_rows, cols = mine.shape
    half = model_rows // 2
    whole = pl.BlockSpec((model_rows, cols), lambda r, *_: (0, 0))
    return pl.pallas_call(
        functools.partial(gram_kernel, wide_ranks),
        out_shape=[
            jax.ShapeDtypeStruct((half, model_rows), dtype)
            for dtype in (jnp.float32, jnp.float32, jnp.bfloat16, jnp.bfloat16)
        ],
        grid_spec=pltpu.PrefetchScalarGridSpec(
            num_scalar_prefetch=2,
            grid=(GROUP,),
            in_specs=[whole, whole],
            out_specs=[pl.BlockSpec(memory_space=pl.ANY)] * GROUP,
            scratch_shapes=[
                pltpu.VMEM((2, half, model_rows), jnp.float32),
                pltpu.VMEM((2, half, model_rows), jnp.bfloat16),
                pltpu.SemaphoreType.DMA((GROUP,)),
            ],
        ),
        name="part_grams",
    )(steps, core, mine, other)


def update_kernel(
    wide_ranks, order, base_ref, rank_ref, scale_ref, weight_ref, back_ref, out_ref, done_ref
):
    layer = pl.program_id(0)
    done_ref[0] = layer
    rows = back_ref.shape[1]
    lane = lax.broadcasted_iota(jnp.int32, (rows, LANES), 1)
    for tile in range(ALL_TILES):
        step = None
        for kind in range(7):
            at = tile - TILE0[kind]
            if not 0 <= at < TILES[kind]:
                continue
            matrix = layer * 7 + kind
            rank = rank_ref[matrix]
            if kind >= FIRST_WIDE:
                source, column = at // WIDE, rank * WIDE + at % WIDE
            else:
                source, column = at, rank_tile(rank, wide_ranks)
            piece = back_ref[
                base_ref[matrix] + chip_at(source, order), :, pl.ds(pl.multiple_of(column * LANES, LANES), LANES)
            ]
            piece = 0.02 * (scale_ref[matrix] * piece.astype(jnp.float32))
            low = STARTS[kind] - tile * LANES
            step = piece if step is None else jnp.where(lane >= low, piece, step)
        where = pl.ds(tile, rows, stride=ALL_TILES)
        out_ref[0, where, :] = weight_ref[0, where, :] - step


def update_weights(wide_ranks, order, plan, ratio, weights, returned):
    layers, rows = weights.shape[:2]
    view = (layers, rows * ALL_TILES, LANES)
    flat_spec = pl.BlockSpec((1,) + view[1:], lambda l, *_: (l, 0, 0))
    out, done = pl.pallas_call(
        functools.partial(update_kernel, wide_ranks, order),
        out_shape=[
            jax.ShapeDtypeStruct(view, jnp.float32),
            jax.ShapeDtypeStruct((1,), jnp.int32),
        ],
        grid_spec=pltpu.PrefetchScalarGridSpec(
            num_scalar_prefetch=3,
            grid=(layers,),
            in_specs=[flat_spec, pl.BlockSpec(returned.shape, lambda l, *_: (0, 0, 0))],
            out_specs=[flat_spec, pl.BlockSpec(memory_space=pltpu.SMEM)],
        ),
        name="update_weights",
    )(plan[3], plan[4], ratio.reshape(-1), weights.reshape(view), returned)
    return out.reshape(weights.shape), done


def swap_cores(value):
    return lax.ppermute(value, "tp", [(0, 1), (1, 0)])


def swap_chips(value, step):
    chips = lax.axis_size("fsdp")
    return lax.ppermute(value, "fsdp", [(i, i ^ step) for i in range(chips)])


def hop(value, first, second):
    chips = lax.axis_size("fsdp")
    pairs = [(2 * i, 2 * (i ^ first)) for i in range(chips)]
    pairs += [(2 * i + 1, 2 * (i ^ second) + 1) for i in range(chips)]
    return lax.ppermute(value, ("fsdp", "tp"), pairs)


def refresh(
    grouping,
    wide_ranks,
    plan,
    grads,
    weights,
    adam_m,
    adam_v,
    stats,
    roots,
    vec_weight,
    vec_grad,
    vec_m,
    vec_v,
):
    chips = lax.axis_size("fsdp")
    chip = lax.axis_index("fsdp")
    core = lax.axis_index("tp").astype(jnp.int32)
    layers = grads.shape[0]
    rows = grads.shape[1]
    model_rows = rows * chips
    cols = slot_tiles(wide_ranks) * LANES
    order = bit_order(grouping, chips)
    steps_to = [chip_at(step, order) for step in range(GROUP)]
    place = place_of(chip, order)
    group_first = place - place % GROUP
    base = chip - chip_at(place % GROUP, order)
    kinds = lax.dynamic_slice(plan[1], (group_first,), (GROUP,))
    places = lax.dynamic_slice(plan[2], (group_first,), (GROUP,))
    own_part = (place % GROUP).astype(jnp.int32)
    owned = jnp.any((places == own_part) & (kinds < NONE))
    core_arg = core.reshape(1)
    steps = places ^ own_part

    outgoing = build_send(wide_ranks, order, plan, grads[:, :, 0, :])
    arrived = lax.all_to_all(outgoing, "fsdp", split_axis=0, concat_axis=0, tiled=True)
    adam_m_new, adam_v_new, adam_part = adam_update(grads[:, :, 0, :], adam_m, adam_v)
    along_x = swap_chips(roots[0], steps_to[1])
    along_y = swap_chips(roots[0], steps_to[2])
    along_x, along_y, adam_part = lax.optimization_barrier((along_x, along_y, adam_part))
    forward = jnp.where(core == 0, along_y, along_x)
    across = hop(forward, steps_to[1], steps_to[2])
    group_roots = [along_x, along_y, across]
    all_roots = []
    for part in [roots[0]] + group_roots:
        all_roots += [part, swap_cores(part)]

    arrived, all_roots, adam_part = lax.optimization_barrier((arrived, all_roots, adam_part))
    gathered = arrived.reshape(model_rows, cols)
    precond, sums = apply_roots(wide_ranks, steps, core_arg, all_roots, gathered)
    precond, gathered_other = lax.optimization_barrier((precond, swap_cores(gathered)))
    returned = lax.all_to_all(
        precond.reshape(chips, rows, cols), "fsdp", split_axis=0, concat_axis=0, tiled=True
    )
    ranks = jnp.arange(GROUP, dtype=jnp.int32)
    is_here = (plan[3] == base)[:, None] & (plan[4][:, None] == ranks[None, :])
    shampoo_part = jnp.sum(jnp.where(is_here, sums[None, :], 0.0), axis=1).reshape(layers, 7)
    totals = jnp.stack([adam_part, shampoo_part])
    totals = totals + swap_cores(totals)
    beside = [totals] + [swap_chips(totals, mask) for mask in steps_to[1:]]
    grams = part_grams(wide_ranks, steps, core_arg, gathered, gathered_other)
    grams, beside = lax.optimization_barrier((grams, beside))
    totals = sum(beside)
    for bit in order[2:]:
        totals = totals + swap_chips(totals, 1 << bit)
    ratio = jnp.sqrt(totals[0]) / (jnp.sqrt(totals[1]) + 1e-06)
    own_term, far_term, near_term, across_term = grams
    near_term = hop(near_term, steps_to[1], steps_to[2])
    across_term = hop(across_term, steps_to[1], steps_to[2])
    far_term = (far_term + across_term.astype(jnp.float32)).astype(jnp.bfloat16)
    far_term = hop(far_term, steps_to[2], steps_to[1])

    weights_new, done = update_weights(wide_ranks, order, plan, ratio, weights, returned)

    stat_term = own_term + near_term.astype(jnp.float32) + far_term.astype(jnp.float32)
    owned = owned & (done[0] >= 0)
    stats_new = jnp.where(owned, 0.9 * stats[0] + 0.1 * stat_term, stats[0])[None]

    vec_float = vec_grad.astype(jnp.float32)
    vec_m_new = 0.9 * vec_m + 0.1 * vec_float
    vec_v_new = 0.99 * vec_v + 0.01 * vec_float * vec_float
    vec_weight_new = vec_weight - 0.02 * vec_m_new / (jnp.sqrt(vec_v_new) + 1e-08)
    return (weights_new, adam_m_new, adam_v_new, stats_new, vec_weight_new, vec_m_new, vec_v_new)


def on_device(owner, *arrays):
    plan = make_plan(owner, lax.axis_size("fsdp"))
    cases = [(grouping, 2) for grouping in GROUPINGS]
    cases += [(GROUPINGS[0], wide_ranks) for wide_ranks in range(3, GROUP + 1)]
    branches = [functools.partial(refresh, *case) for case in cases]
    return lax.switch(plan[5][0], branches, plan, *arrays)


def solution(mesh):
    matrix = P(None, "fsdp", "tp", None)
    slot = P("fsdp", "tp", None)
    vector = P(None, ("fsdp", "tp"))
    return jax.shard_map(
        on_device,
        mesh=mesh,
        in_specs=(P(), matrix, matrix, matrix, matrix, slot, slot, vector, vector, vector, vector),
        out_specs=(matrix, matrix, matrix, slot, vector, vector, vector),
        check_vma=False,
    )
```

```python
import functools

import jax
import jax.numpy as jnp
from jax import lax
from jax.experimental import pallas as pl
from jax.experimental.pallas import tpu as pltpu
from jax.sharding import PartitionSpec as P

FF = 4864
QW = 896
KW = 128
LANES = 128
WIDTHS = [QW // 2, KW // 2, KW // 2, QW // 2, FF // 2, FF // 2, FF // 2]
STARTS = [sum(WIDTHS[:kind]) for kind in range(7)]
TILE0 = [start // LANES for start in STARTS]
TILES = [-(-(start + wide) // LANES) - start // LANES for start, wide in zip(STARTS, WIDTHS)]
HALF = sum(WIDTHS)
ALL_TILES = HALF // LANES
GROUP = 4
WIDE = -(-max(TILES) // GROUP)
FIRST_WIDE = 4
NONE = 7
VMEM_GRANT = 63 * 2**20
GROUPING = (0, 1)


def pick(index, values):
    result = jnp.int32(values[-1])
    for at in range(len(values) - 1):
        result = jnp.where(index == at, values[at], result)
    return result


def bit_order(grouping, chips):
    return list(grouping) + [at for at in range(chips.bit_length() - 1) if at not in grouping]


def chip_at(place, order):
    return sum(((place >> at) & 1) << bit for at, bit in enumerate(order))


def place_of(chip, order):
    return sum(((chip >> bit) & 1) << at for at, bit in enumerate(order))


def row_block(rows):
    return 8 if rows % 8 == 0 else rows


def slot_tiles(wide_ranks, shared):
    return wide_ranks * WIDE + shared


NOWHERE, NOT_LAST, ANYWHERE, FIRST, LAST = range(5)


def is_active(mode, part):
    last = part == GROUP - 1
    return (
        (mode == ANYWHERE)
        | ((mode == NOT_LAST) & jnp.logical_not(last))
        | ((mode == FIRST) & (part == 0))
        | ((mode == LAST) & last)
    )


def plan_kernel(
    cases,
    owner_ref,
    chip_ref,
    layer_ref,
    kind_ref,
    place_ref,
    tile_ref,
    mode_ref,
    base_ref,
    rank_ref,
    column_ref,
    part_ref,
    branch_ref,
    group_ref,
    mat_ref,
    wide_ref,
    spread_ref,
):
    layers = owner_ref.shape[0]
    chips = layer_ref.shape[0]
    order = bit_order(GROUPING, chips)

    def clear(chip, carry):
        mat_ref[chip] = -1
        wide_ref[chip] = 0
        spread_ref[chip] = 0
        return carry

    lax.fori_loop(0, chips, clear, 0)

    def name(matrix, carry):
        layer = matrix // 7
        kind = matrix - layer * 7
        chip = owner_ref[layer, kind]
        mat_ref[chip] = matrix
        wide_ref[chip] = (kind >= FIRST_WIDE).astype(jnp.int32)
        spread_ref[chip] = ((kind == 0) | (kind == FIRST_WIDE - 1)).astype(jnp.int32)
        return carry

    lax.fori_loop(0, layers * 7, name, 0)

    def count(ref, first):
        return sum(ref[chip_at(first + i, order)] for i in range(GROUP))

    most = jnp.int32(2)
    for first in range(0, chips, GROUP):
        most = jnp.maximum(most, count(wide_ref, first))
    spread = jnp.int32(0)
    for first in range(0, chips, GROUP):
        full = count(wide_ref, first) == most
        spread = jnp.maximum(spread, jnp.where(full, count(spread_ref, first), 0))
    branch = jnp.int32(len(cases) - 1)
    for at in reversed(range(len(cases))):
        wide_ranks, shared = cases[at]
        branch = jnp.where((most == wide_ranks) & (spread <= shared), at, branch)
    branch_ref[0] = branch
    wide_ranks = pick(branch, [case[0] for case in cases])
    shared = pick(branch, [case[1] for case in cases])

    def rank_group(group, carry):
        first = group * GROUP
        base = chip_at(first, order)
        members = [base + chip_at(i, order) for i in range(GROUP)]
        wide = [wide_ref[member] for member in members]
        spreads = [spread_ref[member] for member in members]
        before_wide = jnp.int32(0)
        before_spread = sum(wide)
        before_rest = before_spread + sum(spreads)
        free = (wide_ranks - sum(wide)) * WIDE + shared
        for i in range(GROUP):
            matrix = mat_ref[members[i]]
            is_wide = wide[i] == 1
            is_spread = spreads[i] == 1
            rank = jnp.where(is_wide, before_wide, jnp.where(is_spread, before_spread, before_rest))
            before_wide = before_wide + wide[i]
            before_spread = before_spread + spreads[i]
            before_rest = before_rest + 1 - wide[i] - spreads[i]
            there = first + rank
            layer = jnp.maximum(matrix, 0) // 7
            layer_ref[there] = layer
            kind_ref[there] = jnp.where(matrix >= 0, matrix - layer * 7, NONE)
            place_ref[there] = i
            over = rank - sum(wide) - free
            spare = over >= 0
            narrow_tile = jnp.where(spare, over * WIDE + WIDE - 1, sum(wide) * (WIDE - 1) + rank)
            tile = jnp.where(is_wide, rank * WIDE + WIDE - 1, narrow_tile)
            single_mode = jnp.where(matrix < 0, NOWHERE, jnp.where(spare, LAST, FIRST))
            tile_ref[there] = tile
            mode_ref[there] = jnp.where(
                is_wide, NOT_LAST, jnp.where(is_spread, ANYWHERE, single_mode)
            )

            @pl.when(matrix >= 0)
            def _():
                base_ref[matrix] = base
                rank_ref[matrix] = rank
                column_ref[matrix] = jnp.where(is_wide, rank * WIDE, tile)
                part_ref[matrix] = jnp.where(spare, GROUP - 1, 0)

        return carry

    lax.fori_loop(0, chips // GROUP, rank_group, 0)

    place = place_of(chip_ref[0], order)
    part = place % GROUP
    for rank in range(GROUP):
        there = place - part + rank
        group_ref[0, rank] = place_ref[there] ^ part
        group_ref[1, rank] = kind_ref[there]
        group_ref[2, rank] = tile_ref[there]
        group_ref[3, rank] = is_active(mode_ref[there], part).astype(jnp.int32)
    group_ref[4, 0] = (mat_ref[chip_ref[0]] >= 0).astype(jnp.int32)


def make_plan(cases, owner, chips):
    matrices = owner.shape[0] * 7
    sizes = [chips] * 5 + [matrices] * 4 + [1]
    smem = pl.BlockSpec(memory_space=pltpu.SMEM)
    return pl.pallas_call(
        functools.partial(plan_kernel, cases),
        out_shape=[jax.ShapeDtypeStruct((size,), jnp.int32) for size in sizes]
        + [jax.ShapeDtypeStruct((5, GROUP), jnp.int32)],
        in_specs=[smem] * 2,
        out_specs=[smem] * (len(sizes) + 1),
        scratch_shapes=[pltpu.SMEM((chips,), jnp.int32)] * 3,
        name="plan",
    )(owner, lax.axis_index("fsdp").astype(jnp.int32).reshape(1))


def send_kernel(
    order, layer_ref, kind_ref, tile_ref, mode_ref, grad_ref, out_hbm, out_ref, out_sem
):
    group = pl.program_id(0) * GROUP
    chips = out_ref.shape[0]
    rows = grad_ref.shape[1]
    lane = lax.broadcasted_iota(jnp.int32, (rows, LANES), 1)

    def tile_at(at):
        return pl.ds(pl.multiple_of(at * LANES, LANES), LANES)

    def fill(part, carry):
        place = group + part
        out_ref[place] = jnp.zeros(out_ref.shape[1:], jnp.bfloat16)
        for rank in range(GROUP):
            layer = layer_ref[group + rank]
            kind = kind_ref[group + rank]
            first = pick(kind, TILE0 + [0])
            is_wide = (kind >= FIRST_WIDE) & (kind < NONE)
            mode = mode_ref[group + rank]

            @pl.when(is_wide)
            def _():
                for at in range(WIDE - 1):
                    source = first + part * WIDE + at
                    out_ref[place, :, tile_at(rank * WIDE + at)] = grad_ref[
                        layer, :, tile_at(source)
                    ]

            @pl.when(is_active(mode, part))
            def _():
                on_part = jnp.where(mode == ANYWHERE, part, 0)
                source = first + jnp.where(is_wide, part * WIDE + WIDE - 1, on_part)
                low = pick(kind, STARTS + [0])
                high = low + pick(kind, WIDTHS + [0])
                column = lane + source * LANES
                value = grad_ref[layer, :, tile_at(source)].astype(jnp.float32)
                value = jnp.where((column >= low) & (column < high), value, 0.0)
                out_ref[place, :, tile_at(tile_ref[group + rank])] = value.astype(jnp.bfloat16)

        out_copy(place).start()
        return carry

    def out_copy(place):
        return pltpu.make_async_copy(
            out_ref.at[place], out_hbm.at[chip_at(place, order)], out_sem.at[place]
        )

    def wait(place, carry):
        out_copy(place).wait()
        return carry

    lax.fori_loop(0, GROUP, fill, 0)

    @pl.when(pl.program_id(0) == pl.num_programs(0) - 1)
    def _():
        lax.fori_loop(0, chips, wait, 0)


def build_send(tiles, order, plan, grads):
    layers, rows, _ = grads.shape
    chips = plan[0].shape[0]
    cols = tiles * LANES
    return pl.pallas_call(
        functools.partial(send_kernel, order),
        out_shape=jax.ShapeDtypeStruct((chips, rows, cols), jnp.bfloat16),
        grid_spec=pltpu.PrefetchScalarGridSpec(
            num_scalar_prefetch=4,
            grid=(chips // GROUP,),
            in_specs=[pl.BlockSpec((layers, rows, HALF), lambda g, *_: (0, 0, 0))],
            out_specs=pl.BlockSpec(memory_space=pl.ANY),
            scratch_shapes=[
                pltpu.VMEM((chips, rows, cols), jnp.bfloat16),
                pltpu.SemaphoreType.DMA((chips,)),
            ],
        ),
        name="build_send",
    )(plan[0], plan[1], plan[3], plan[4], grads)


def adam_kernel(grad_ref, m_ref, v_ref, m_out, v_out, sum_ref, grad_flat, total_ref):
    layer = pl.program_id(0)
    block = grad_ref.shape[1]
    for tile in range(ALL_TILES):
        piece = grad_ref[0, :, tile * LANES : (tile + 1) * LANES]
        grad_flat[pl.ds(tile, block, stride=ALL_TILES), :] = piece.astype(jnp.float32)
    grad = grad_flat[...]
    m_new = 0.9 * m_ref[0] + 0.1 * grad
    v_new = 0.99 * v_ref[0] + 0.01 * grad * grad
    m_out[0] = m_new
    v_out[0] = v_new
    step = m_new / (jnp.sqrt(v_new) + 1e-08)
    square = step * step

    @pl.when(pl.program_id(1) == 0)
    def _():
        total_ref[...] = square

    @pl.when(pl.program_id(1) > 0)
    def _():
        total_ref[...] += square

    @pl.when(pl.program_id(1) == pl.num_programs(1) - 1)
    def _():
        by_column = total_ref[0:ALL_TILES, :]
        for row in range(1, block):
            by_column = by_column + total_ref[row * ALL_TILES : (row + 1) * ALL_TILES, :]
        column = lax.broadcasted_iota(jnp.int32, by_column.shape, 0) * LANES
        column = column + lax.broadcasted_iota(jnp.int32, by_column.shape, 1)
        for kind in range(7):
            keep = (column >= STARTS[kind]) & (column < STARTS[kind] + WIDTHS[kind])
            sum_ref[layer, kind] = jnp.sum(jnp.where(keep, by_column, 0.0))


def adam_update(grads, adam_m, adam_v):
    layers, rows, _ = grads.shape
    block = row_block(rows)
    blocks = rows // block
    view = (layers * blocks, block * ALL_TILES, LANES)
    flat_spec = pl.BlockSpec((1,) + view[1:], lambda l, r: (l * blocks + r, 0, 0))
    flat = jax.ShapeDtypeStruct(view, jnp.float32)
    count = layers * rows * HALF
    m_new, v_new, sums = pl.pallas_call(
        adam_kernel,
        out_shape=[flat, flat, jax.ShapeDtypeStruct((layers, 7), jnp.float32)],
        grid_spec=pltpu.PrefetchScalarGridSpec(
            num_scalar_prefetch=0,
            grid=(layers, blocks),
            in_specs=[pl.BlockSpec((1, block, HALF), lambda l, r: (l, r, 0)), flat_spec, flat_spec],
            out_specs=[flat_spec, flat_spec, pl.BlockSpec(memory_space=pltpu.SMEM)],
            scratch_shapes=[pltpu.VMEM(view[1:], jnp.float32), pltpu.VMEM(view[1:], jnp.float32)],
        ),
        cost_estimate=pl.CostEstimate(
            flops=12 * count, bytes_accessed=18 * count, transcendentals=2 * count
        ),
        compiler_params=pltpu.CompilerParams(vmem_limit_bytes=VMEM_GRANT),
        name="adam_update",
    )(grads, adam_m.reshape(view), adam_v.reshape(view))
    return m_new.reshape(adam_m.shape), v_new.reshape(adam_v.shape), sums


def apply_kernel(wide_ranks, group_ref, core_ref, *refs):
    root_refs = refs[: 2 * GROUP]
    grad_hbm, out_hbm, sum_ref, root_buf, grad_buf, out_buf, root_sem, grad_sem, out_sem = refs[
        2 * GROUP :
    ]
    half = root_refs[0].shape[0]
    core = core_ref[0]
    tail = grad_buf.shape[1] - wide_ranks * WIDE * LANES

    def tiles_at(at, tiles):
        return pl.ds(pl.multiple_of(at * LANES, LANES), tiles * LANES)

    def is_wide(rank):
        return (group_ref[1, rank] >= FIRST_WIDE) & (group_ref[1, rank] < NONE)

    def root_copy(step, rank, side):
        at = pl.multiple_of((core if side == 0 else 1 - core) * half, half)
        return pltpu.make_async_copy(
            root_refs[2 * step + side],
            root_buf.at[rank, pl.ds(at, half), :],
            root_sem.at[rank, side],
        )

    def part_copy(source, target, part, sem):
        return pltpu.make_async_copy(source.at[:, part], target.at[:, part], sem)

    def grad_copy(rank):
        part = tiles_at(rank * WIDE, WIDE)
        return part_copy(grad_hbm, grad_buf, part, grad_sem.at[rank])

    def out_copy(rank):
        part = tiles_at(rank * WIDE, WIDE - 1)
        return part_copy(out_buf, out_hbm, part, out_sem.at[rank])

    def single_copy(rank):
        part = tiles_at(rank * WIDE + WIDE - 1, 1)
        return part_copy(out_buf, out_hbm, part, out_sem.at[GROUP + rank])

    def tail_copy(source, target, sem):
        return part_copy(source, target, pl.ds(wide_ranks * WIDE * LANES, tail), sem)

    for rank in range(GROUP):
        if rank < wide_ranks:
            grad_copy(rank).start()
        elif rank == wide_ranks and tail:
            tail_copy(grad_hbm, grad_buf, grad_sem.at[rank]).start()
        for step in range(GROUP):

            @pl.when(group_ref[0, rank] == step)
            def _():
                root_copy(step, rank, 0).start()
                root_copy(step, rank, 1).start()

    def run(rank, part):
        def side(at, total):
            rows = pl.ds(pl.multiple_of(at * half, half), half)
            value = jnp.dot(
                root_buf[rank, rows, :], grad_buf[:, part], preferred_element_type=jnp.float32
            )
            value = value.astype(jnp.bfloat16)
            out_buf[rows, part] = value
            value = value.astype(jnp.float32)
            return total + jnp.sum((value * value).reshape(half // 8, 8, -1), axis=0)

        total = lax.fori_loop(0, 2, side, jnp.zeros((8, part.size), jnp.float32))
        sum_ref[rank] += jnp.sum(total)

    def root_wait(rank):
        root_copy(0, rank, 0).wait()
        root_copy(0, rank, 1).wait()

    def wide(rank, carry):
        grad_copy(rank).wait()
        root_wait(rank)
        sum_ref[rank] = jnp.float32(0.0)

        @pl.when(is_wide(rank))
        def _():
            run(rank, tiles_at(rank * WIDE, WIDE - 1))
            out_copy(rank).start()

        return carry

    lax.fori_loop(0, wide_ranks, wide, 0)
    if tail:
        tail_copy(grad_hbm, grad_buf, grad_sem.at[wide_ranks]).wait()

    def single(rank, carry):
        @pl.when(rank >= wide_ranks)
        def _():
            root_wait(rank)
            sum_ref[rank] = jnp.float32(0.0)

        @pl.when(group_ref[3, rank] == 1)
        def _():
            run(rank, tiles_at(group_ref[2, rank], 1))

        return carry

    lax.fori_loop(0, GROUP, single, 0)
    if tail:
        tail_copy(out_buf, out_hbm, out_sem.at[2 * GROUP]).start()
    for rank in range(wide_ranks):
        single_copy(rank).start()

        @pl.when(jnp.logical_not(is_wide(rank)))
        def _():
            out_copy(rank).start()

    for rank in range(wide_ranks):
        single_copy(rank).wait()
        out_copy(rank).wait()
    if tail:
        tail_copy(out_buf, out_hbm, out_sem.at[2 * GROUP]).wait()


def apply_roots(wide_ranks, group, roots, gathered):
    half, model_rows = roots[0].shape
    cols = gathered.shape[1]
    anywhere = pl.BlockSpec(memory_space=pl.ANY)
    return pl.pallas_call(
        functools.partial(apply_kernel, wide_ranks),
        out_shape=[
            jax.ShapeDtypeStruct((model_rows, cols), jnp.bfloat16),
            jax.ShapeDtypeStruct((GROUP,), jnp.float32),
        ],
        grid_spec=pltpu.PrefetchScalarGridSpec(
            num_scalar_prefetch=2,
            grid=(1,),
            in_specs=[anywhere] * (2 * GROUP + 1),
            out_specs=[anywhere, pl.BlockSpec(memory_space=pltpu.SMEM)],
            scratch_shapes=[
                pltpu.VMEM((GROUP, model_rows, model_rows), jnp.bfloat16),
                pltpu.VMEM((model_rows, cols), jnp.bfloat16),
                pltpu.VMEM((model_rows, cols), jnp.bfloat16),
                pltpu.SemaphoreType.DMA((GROUP, 2)),
                pltpu.SemaphoreType.DMA((GROUP + 1,)),
                pltpu.SemaphoreType.DMA((2 * GROUP + 1,)),
            ],
        ),
        compiler_params=pltpu.CompilerParams(vmem_limit_bytes=VMEM_GRANT),
        name="apply_roots",
    )(*group, *roots, gathered)


def gram_kernel(group_ref, core_ref, mine_ref, other_ref, *refs):
    out_refs = refs[:GROUP]
    keep_buf, send_buf, total_ref, out_sem = refs[GROUP:]
    rank = pl.program_id(0)
    half = keep_buf.shape[1]
    core = core_ref[0]
    step = group_ref[0, rank]
    near = step == 1 + core
    far = step == 2 - core

    total_ref[...] = jnp.zeros(total_ref.shape, jnp.float32)

    def run(tile, tiles):
        columns = pl.ds(pl.multiple_of(tile * LANES, LANES), tiles * LANES)
        rows = pl.ds(pl.multiple_of(core * half, half), half)
        for grad_ref in (mine_ref, other_ref):
            total_ref[...] += lax.dot_general(
                grad_ref[rows, columns],
                grad_ref[:, columns],
                (((1,), (1,)), ((), ())),
                preferred_element_type=jnp.float32,
            )

    @pl.when((group_ref[1, rank] >= FIRST_WIDE) & (group_ref[1, rank] < NONE))
    def _():
        run(rank * WIDE, WIDE - 1)

    @pl.when(group_ref[3, rank] == 1)
    def _():
        run(group_ref[2, rank], 1)

    @pl.when((step == 0) | far)
    def _():
        keep_buf[jnp.minimum(step, 1)] = total_ref[...]

    @pl.when(near | (step == 3))
    def _():
        send_buf[jnp.maximum(step, 2) - 2] = total_ref[...].astype(jnp.bfloat16)

    def out_copy(at):
        source = keep_buf.at[at] if at < 2 else send_buf.at[at - 2]
        return pltpu.make_async_copy(source, out_refs[at], out_sem.at[at])

    @pl.when(step == 0)
    def _():
        out_copy(0).start()

    @pl.when(far)
    def _():
        out_copy(1).start()

    @pl.when(near)
    def _():
        out_copy(2).start()

    @pl.when(step == 3)
    def _():
        out_copy(3).start()

    @pl.when(rank == GROUP - 1)
    def _():
        for at in range(GROUP):
            out_copy(at).wait()


def part_grams(group, mine, other):
    model_rows, cols = mine.shape
    half = model_rows // 2
    whole = pl.BlockSpec((model_rows, cols), lambda r, *_: (0, 0))
    return pl.pallas_call(
        gram_kernel,
        out_shape=[
            jax.ShapeDtypeStruct((half, model_rows), dtype)
            for dtype in (jnp.float32, jnp.float32, jnp.bfloat16, jnp.bfloat16)
        ],
        grid_spec=pltpu.PrefetchScalarGridSpec(
            num_scalar_prefetch=2,
            grid=(GROUP,),
            in_specs=[whole, whole],
            out_specs=[pl.BlockSpec(memory_space=pl.ANY)] * GROUP,
            scratch_shapes=[
                pltpu.VMEM((2, half, model_rows), jnp.float32),
                pltpu.VMEM((2, half, model_rows), jnp.bfloat16),
                pltpu.VMEM((half, model_rows), jnp.float32),
                pltpu.SemaphoreType.DMA((GROUP,)),
            ],
        ),
        compiler_params=pltpu.CompilerParams(vmem_limit_bytes=VMEM_GRANT),
        name="part_grams",
    )(*group, mine, other)


def update_kernel(
    order, base_ref, column_ref, part_ref, scale_ref, weight_ref, back_ref, out_ref, done_ref
):
    layer = pl.program_id(0)
    done_ref[0] = layer
    rows = back_ref.shape[1]
    lane = lax.broadcasted_iota(jnp.int32, (rows, LANES), 1)
    for tile in range(ALL_TILES):
        step = None
        for kind in range(7):
            at = tile - TILE0[kind]
            if not 0 <= at < TILES[kind]:
                continue
            matrix = layer * 7 + kind
            source, column = base_ref[matrix], column_ref[matrix]
            if kind >= FIRST_WIDE:
                source, column = source + chip_at(at // WIDE, order), column + at % WIDE
            elif TILES[kind] > 1:
                source = source + chip_at(at, order)
            else:
                source = source + chip_at(part_ref[matrix], order)
            piece = back_ref[source, :, pl.ds(pl.multiple_of(column * LANES, LANES), LANES)]
            piece = 0.02 * (scale_ref[matrix] * piece.astype(jnp.float32))
            low = STARTS[kind] - tile * LANES
            step = piece if step is None else jnp.where(lane >= low, piece, step)
        where = pl.ds(tile, rows, stride=ALL_TILES)
        out_ref[0, where, :] = weight_ref[0, where, :] - step


def update_weights(order, plan, ratio, weights, returned):
    layers, rows = weights.shape[:2]
    view = (layers, rows * ALL_TILES, LANES)
    flat_spec = pl.BlockSpec((1,) + view[1:], lambda l, *_: (l, 0, 0))
    out, done = pl.pallas_call(
        functools.partial(update_kernel, order),
        out_shape=[
            jax.ShapeDtypeStruct(view, jnp.float32),
            jax.ShapeDtypeStruct((1,), jnp.int32),
        ],
        grid_spec=pltpu.PrefetchScalarGridSpec(
            num_scalar_prefetch=4,
            grid=(layers,),
            in_specs=[flat_spec, pl.BlockSpec(returned.shape, lambda l, *_: (0, 0, 0))],
            out_specs=[flat_spec, pl.BlockSpec(memory_space=pltpu.SMEM)],
        ),
        compiler_params=pltpu.CompilerParams(vmem_limit_bytes=VMEM_GRANT),
        name="update_weights",
    )(plan[5], plan[7], plan[8], ratio.reshape(-1), weights.reshape(view), returned)
    return out.reshape(weights.shape), done


def swap_cores(value):
    return lax.ppermute(value, "tp", [(0, 1), (1, 0)])


def swap_chips(value, step):
    chips = lax.axis_size("fsdp")
    return lax.ppermute(value, "fsdp", [(i, i ^ step) for i in range(chips)])


def hop(value, first, second):
    chips = lax.axis_size("fsdp")
    pairs = [(2 * i, 2 * (i ^ first)) for i in range(chips)]
    pairs += [(2 * i + 1, 2 * (i ^ second) + 1) for i in range(chips)]
    return lax.ppermute(value, ("fsdp", "tp"), pairs)


def refresh(
    wide_ranks,
    shared,
    plan,
    grads,
    weights,
    adam_m,
    adam_v,
    stats,
    roots,
    vec_weight,
    vec_grad,
    vec_m,
    vec_v,
):
    chips = lax.axis_size("fsdp")
    chip = lax.axis_index("fsdp")
    core = lax.axis_index("tp").astype(jnp.int32)
    layers = grads.shape[0]
    rows = grads.shape[1]
    model_rows = rows * chips
    tiles = slot_tiles(wide_ranks, shared)
    cols = tiles * LANES
    order = bit_order(GROUPING, chips)
    steps_to = [chip_at(step, order) for step in range(GROUP)]
    place = place_of(chip, order)
    base = chip - chip_at(place % GROUP, order)
    group = (plan[10], core.reshape(1))

    outgoing = build_send(tiles, order, plan, grads[:, :, 0, :])
    arrived = lax.all_to_all(outgoing, "fsdp", split_axis=0, concat_axis=0, tiled=True)
    along_x = swap_chips(roots[0], steps_to[1])
    along_y = swap_chips(roots[0], steps_to[2])
    along_x, along_y, adam_grads = lax.optimization_barrier((along_x, along_y, grads[:, :, 0, :]))
    adam_m_new, adam_v_new, adam_part = adam_update(adam_grads, adam_m, adam_v)
    forward = jnp.where(core == 0, along_y, along_x)
    across = hop(forward, steps_to[1], steps_to[2])
    across, adam_part = lax.optimization_barrier((across, adam_part))
    group_roots = [along_x, along_y, across]
    all_roots = []
    for part in [roots[0]] + group_roots:
        all_roots += [part, swap_cores(part)]

    arrived, all_roots, adam_part = lax.optimization_barrier((arrived, all_roots, adam_part))
    gathered = arrived.reshape(model_rows, cols)
    precond, sums = apply_roots(wide_ranks, group, all_roots, gathered)
    precond, gathered_other = lax.optimization_barrier((precond, swap_cores(gathered)))
    returned = lax.all_to_all(
        precond.reshape(chips, rows, cols), "fsdp", split_axis=0, concat_axis=0, tiled=True
    )
    ranks = jnp.arange(GROUP, dtype=jnp.int32)
    is_here = (plan[5] == base)[:, None] & (plan[6][:, None] == ranks[None, :])
    shampoo_part = jnp.sum(jnp.where(is_here, sums[None, :], 0.0), axis=1).reshape(layers, 7)
    totals = jnp.stack([adam_part, shampoo_part])
    totals = totals + swap_cores(totals)
    beside = [totals] + [swap_chips(totals, mask) for mask in steps_to[1:]]
    grams = part_grams(group, gathered, gathered_other)
    grams, beside = lax.optimization_barrier((grams, beside))
    totals = sum(beside)
    for bit in order[2:]:
        totals = totals + swap_chips(totals, 1 << bit)
    ratio = jnp.sqrt(totals[0]) / (jnp.sqrt(totals[1]) + 1e-06)
    own_term, far_term, near_term, across_term = grams
    near_term = hop(near_term, steps_to[1], steps_to[2])
    across_term = hop(across_term, steps_to[1], steps_to[2])
    far_term = (far_term + across_term.astype(jnp.float32)).astype(jnp.bfloat16)
    far_term = hop(far_term, steps_to[2], steps_to[1])

    weights_new, done = update_weights(order, plan, ratio, weights, returned)

    stat_term = own_term + near_term.astype(jnp.float32) + far_term.astype(jnp.float32)
    owned = (plan[10][4, 0] == 1) & (done[0] >= 0)
    stats_new = jnp.where(owned, 0.9 * stats[0] + 0.1 * stat_term, stats[0])[None]

    vec_float = vec_grad.astype(jnp.float32)
    vec_m_new = 0.9 * vec_m + 0.1 * vec_float
    vec_v_new = 0.99 * vec_v + 0.01 * vec_float * vec_float
    vec_weight_new = vec_weight - 0.02 * vec_m_new / (jnp.sqrt(vec_v_new) + 1e-08)
    return (weights_new, adam_m_new, adam_v_new, stats_new, vec_weight_new, vec_m_new, vec_v_new)


def on_device(owner, *arrays):
    cases = [(2, 1), (2, 2), (3, 1), (4, 0)]
    plan = make_plan(cases, owner, lax.axis_size("fsdp"))
    branches = [functools.partial(refresh, *case) for case in cases]
    return lax.switch(plan[9][0], branches, plan, *arrays)


def solution(mesh):
    matrix = P(None, "fsdp", "tp", None)
    slot = P("fsdp", "tp", None)
    vector = P(None, ("fsdp", "tp"))
    return jax.shard_map(
        on_device,
        mesh=mesh,
        in_specs=(P(), matrix, matrix, matrix, matrix, slot, slot, vector, vector, vector, vector),
        out_specs=(matrix, matrix, matrix, slot, vector, vector, vector),
        check_vma=False,
    )
```

```python
import functools

import jax
import jax.numpy as jnp
from jax import lax
from jax.experimental import pallas as pl
from jax.experimental.pallas import tpu as pltpu
from jax.sharding import PartitionSpec as P

FF = 4864
QW = 896
KW = 128
LANES = 128
WIDTHS = [QW // 2, KW // 2, KW // 2, QW // 2, FF // 2, FF // 2, FF // 2]
STARTS = [sum(WIDTHS[:kind]) for kind in range(7)]
TILE0 = [start // LANES for start in STARTS]
TILES = [-(-(start + wide) // LANES) - start // LANES for start, wide in zip(STARTS, WIDTHS)]
HALF = sum(WIDTHS)
ALL_TILES = HALF // LANES
GROUP = 4
WIDE = -(-max(TILES) // GROUP)
FIRST_WIDE = 4
NONE = 7
VMEM_GRANT = 63 * 2**20
GROUPING = (0, 1)


def pick(index, values):
    result = jnp.int32(values[-1])
    for at in range(len(values) - 1):
        result = jnp.where(index == at, values[at], result)
    return result


def bit_order(grouping, chips):
    return list(grouping) + [at for at in range(chips.bit_length() - 1) if at not in grouping]


def chip_at(place, order):
    return sum(((place >> at) & 1) << bit for at, bit in enumerate(order))


def place_of(chip, order):
    return sum(((chip >> bit) & 1) << at for at, bit in enumerate(order))


def row_block(rows):
    return 8 if rows % 8 == 0 else rows


def slot_tiles(wide_ranks, shared):
    return wide_ranks * WIDE + shared


NOWHERE, NOT_LAST, ANYWHERE, FIRST, LAST = range(5)


def is_active(mode, part):
    last = part == GROUP - 1
    return (
        (mode == ANYWHERE)
        | ((mode == NOT_LAST) & jnp.logical_not(last))
        | ((mode == FIRST) & (part == 0))
        | ((mode == LAST) & last)
    )


def plan_kernel(
    cases,
    owner_ref,
    chip_ref,
    layer_ref,
    kind_ref,
    place_ref,
    tile_ref,
    mode_ref,
    base_ref,
    rank_ref,
    column_ref,
    part_ref,
    branch_ref,
    group_ref,
    mat_ref,
    wide_ref,
    spread_ref,
):
    layers = owner_ref.shape[0]
    chips = layer_ref.shape[0]
    order = bit_order(GROUPING, chips)

    def clear(chip, carry):
        mat_ref[chip] = -1
        wide_ref[chip] = 0
        spread_ref[chip] = 0
        return carry

    lax.fori_loop(0, chips, clear, 0)

    def name(matrix, carry):
        layer = matrix // 7
        kind = matrix - layer * 7
        chip = owner_ref[layer, kind]
        mat_ref[chip] = matrix
        wide_ref[chip] = (kind >= FIRST_WIDE).astype(jnp.int32)
        spread_ref[chip] = ((kind == 0) | (kind == FIRST_WIDE - 1)).astype(jnp.int32)
        return carry

    lax.fori_loop(0, layers * 7, name, 0)

    def count(ref, first):
        return sum(ref[chip_at(first + i, order)] for i in range(GROUP))

    most = jnp.int32(2)
    for first in range(0, chips, GROUP):
        most = jnp.maximum(most, count(wide_ref, first))
    spread = jnp.int32(0)
    for first in range(0, chips, GROUP):
        full = count(wide_ref, first) == most
        spread = jnp.maximum(spread, jnp.where(full, count(spread_ref, first), 0))
    branch = jnp.int32(len(cases) - 1)
    for at in reversed(range(len(cases))):
        wide_ranks, shared = cases[at]
        branch = jnp.where((most == wide_ranks) & (spread <= shared), at, branch)
    branch_ref[0] = branch
    wide_ranks = pick(branch, [case[0] for case in cases])
    shared = pick(branch, [case[1] for case in cases])

    def rank_group(group, carry):
        first = group * GROUP
        base = chip_at(first, order)
        members = [base + chip_at(i, order) for i in range(GROUP)]
        wide = [wide_ref[member] for member in members]
        spreads = [spread_ref[member] for member in members]
        before_wide = jnp.int32(0)
        before_spread = sum(wide)
        before_rest = before_spread + sum(spreads)
        free = (wide_ranks - sum(wide)) * WIDE + shared
        for i in range(GROUP):
            matrix = mat_ref[members[i]]
            is_wide = wide[i] == 1
            is_spread = spreads[i] == 1
            rank = jnp.where(is_wide, before_wide, jnp.where(is_spread, before_spread, before_rest))
            before_wide = before_wide + wide[i]
            before_spread = before_spread + spreads[i]
            before_rest = before_rest + 1 - wide[i] - spreads[i]
            there = first + rank
            layer = jnp.maximum(matrix, 0) // 7
            layer_ref[there] = layer
            kind_ref[there] = jnp.where(matrix >= 0, matrix - layer * 7, NONE)
            place_ref[there] = i
            over = rank - sum(wide) - free
            spare = over >= 0
            narrow_tile = jnp.where(spare, over * WIDE + WIDE - 1, sum(wide) * (WIDE - 1) + rank)
            tile = jnp.where(is_wide, rank * WIDE + WIDE - 1, narrow_tile)
            single_mode = jnp.where(matrix < 0, NOWHERE, jnp.where(spare, LAST, FIRST))
            tile_ref[there] = tile
            mode_ref[there] = jnp.where(
                is_wide, NOT_LAST, jnp.where(is_spread, ANYWHERE, single_mode)
            )

            @pl.when(matrix >= 0)
            def _():
                base_ref[matrix] = base
                rank_ref[matrix] = rank
                column_ref[matrix] = jnp.where(is_wide, rank * WIDE, tile)
                part_ref[matrix] = jnp.where(spare, GROUP - 1, 0)

        return carry

    lax.fori_loop(0, chips // GROUP, rank_group, 0)

    place = place_of(chip_ref[0], order)
    part = place % GROUP
    for rank in range(GROUP):
        there = place - part + rank
        group_ref[0, rank] = place_ref[there] ^ part
        group_ref[1, rank] = kind_ref[there]
        group_ref[2, rank] = tile_ref[there]
        group_ref[3, rank] = is_active(mode_ref[there], part).astype(jnp.int32)
    group_ref[4, 0] = (mat_ref[chip_ref[0]] >= 0).astype(jnp.int32)


def make_plan(cases, owner, chips):
    matrices = owner.shape[0] * 7
    sizes = [chips] * 5 + [matrices] * 4 + [1]
    smem = pl.BlockSpec(memory_space=pltpu.SMEM)
    return pl.pallas_call(
        functools.partial(plan_kernel, cases),
        out_shape=[jax.ShapeDtypeStruct((size,), jnp.int32) for size in sizes]
        + [jax.ShapeDtypeStruct((5, GROUP), jnp.int32)],
        in_specs=[smem] * 2,
        out_specs=[smem] * (len(sizes) + 1),
        scratch_shapes=[pltpu.SMEM((chips,), jnp.int32)] * 3,
        name="plan",
    )(owner, lax.axis_index("fsdp").astype(jnp.int32).reshape(1))


def send_kernel(
    order, layer_ref, kind_ref, tile_ref, mode_ref, grad_ref, out_hbm, out_ref, out_sem
):
    group = pl.program_id(0) * GROUP
    chips = out_ref.shape[0]
    rows = grad_ref.shape[1]
    lane = lax.broadcasted_iota(jnp.int32, (rows, LANES), 1)

    def tile_at(at):
        return pl.ds(pl.multiple_of(at * LANES, LANES), LANES)

    def fill(part, carry):
        place = group + part
        out_ref[place] = jnp.zeros(out_ref.shape[1:], jnp.bfloat16)
        for rank in range(GROUP):
            layer = layer_ref[group + rank]
            kind = kind_ref[group + rank]
            first = pick(kind, TILE0 + [0])
            is_wide = (kind >= FIRST_WIDE) & (kind < NONE)
            mode = mode_ref[group + rank]

            @pl.when(is_wide)
            def _():
                for at in range(WIDE - 1):
                    source = first + part * WIDE + at
                    out_ref[place, :, tile_at(rank * WIDE + at)] = grad_ref[
                        layer, :, tile_at(source)
                    ]

            @pl.when(is_active(mode, part))
            def _():
                on_part = jnp.where(mode == ANYWHERE, part, 0)
                source = first + jnp.where(is_wide, part * WIDE + WIDE - 1, on_part)
                low = pick(kind, STARTS + [0])
                high = low + pick(kind, WIDTHS + [0])
                column = lane + source * LANES
                value = grad_ref[layer, :, tile_at(source)].astype(jnp.float32)
                value = jnp.where((column >= low) & (column < high), value, 0.0)
                out_ref[place, :, tile_at(tile_ref[group + rank])] = value.astype(jnp.bfloat16)

        out_copy(place).start()
        return carry

    def out_copy(place):
        return pltpu.make_async_copy(
            out_ref.at[place], out_hbm.at[chip_at(place, order)], out_sem.at[place]
        )

    def wait(place, carry):
        out_copy(place).wait()
        return carry

    lax.fori_loop(0, GROUP, fill, 0)

    @pl.when(pl.program_id(0) == pl.num_programs(0) - 1)
    def _():
        lax.fori_loop(0, chips, wait, 0)


def build_send(tiles, order, plan, grads):
    layers, rows, _ = grads.shape
    chips = plan[0].shape[0]
    cols = tiles * LANES
    return pl.pallas_call(
        functools.partial(send_kernel, order),
        out_shape=jax.ShapeDtypeStruct((chips, rows, cols), jnp.bfloat16),
        grid_spec=pltpu.PrefetchScalarGridSpec(
            num_scalar_prefetch=4,
            grid=(chips // GROUP,),
            in_specs=[pl.BlockSpec((layers, rows, HALF), lambda g, *_: (0, 0, 0))],
            out_specs=pl.BlockSpec(memory_space=pl.ANY),
            scratch_shapes=[
                pltpu.VMEM((chips, rows, cols), jnp.bfloat16),
                pltpu.SemaphoreType.DMA((chips,)),
            ],
        ),
        name="build_send",
    )(plan[0], plan[1], plan[3], plan[4], grads)


def adam_kernel(grad_ref, m_ref, v_ref, m_out, v_out, sum_ref, grad_flat, total_ref):
    layer = pl.program_id(0)
    block = grad_ref.shape[1]
    for tile in range(ALL_TILES):
        piece = grad_ref[0, :, tile * LANES : (tile + 1) * LANES]
        grad_flat[pl.ds(tile, block, stride=ALL_TILES), :] = piece.astype(jnp.float32)
    grad = grad_flat[...]
    m_new = 0.9 * m_ref[0] + 0.1 * grad
    v_new = 0.99 * v_ref[0] + 0.01 * grad * grad
    m_out[0] = m_new
    v_out[0] = v_new
    step = m_new / (jnp.sqrt(v_new) + 1e-08)
    square = step * step

    @pl.when(pl.program_id(1) == 0)
    def _():
        total_ref[...] = square

    @pl.when(pl.program_id(1) > 0)
    def _():
        total_ref[...] += square

    @pl.when(pl.program_id(1) == pl.num_programs(1) - 1)
    def _():
        by_column = total_ref[0:ALL_TILES, :]
        for row in range(1, block):
            by_column = by_column + total_ref[row * ALL_TILES : (row + 1) * ALL_TILES, :]
        column = lax.broadcasted_iota(jnp.int32, by_column.shape, 0) * LANES
        column = column + lax.broadcasted_iota(jnp.int32, by_column.shape, 1)
        for kind in range(7):
            keep = (column >= STARTS[kind]) & (column < STARTS[kind] + WIDTHS[kind])
            sum_ref[layer, kind] = jnp.sum(jnp.where(keep, by_column, 0.0))


def adam_update(grads, adam_m, adam_v):
    layers, rows, _ = grads.shape
    block = row_block(rows)
    blocks = rows // block
    view = (layers * blocks, block * ALL_TILES, LANES)
    flat_spec = pl.BlockSpec((1,) + view[1:], lambda l, r: (l * blocks + r, 0, 0))
    flat = jax.ShapeDtypeStruct(view, jnp.float32)
    count = layers * rows * HALF
    m_new, v_new, sums = pl.pallas_call(
        adam_kernel,
        out_shape=[flat, flat, jax.ShapeDtypeStruct((layers, 7), jnp.float32)],
        grid_spec=pltpu.PrefetchScalarGridSpec(
            num_scalar_prefetch=0,
            grid=(layers, blocks),
            in_specs=[pl.BlockSpec((1, block, HALF), lambda l, r: (l, r, 0)), flat_spec, flat_spec],
            out_specs=[flat_spec, flat_spec, pl.BlockSpec(memory_space=pltpu.SMEM)],
            scratch_shapes=[pltpu.VMEM(view[1:], jnp.float32), pltpu.VMEM(view[1:], jnp.float32)],
        ),
        cost_estimate=pl.CostEstimate(
            flops=12 * count, bytes_accessed=18 * count, transcendentals=2 * count
        ),
        compiler_params=pltpu.CompilerParams(vmem_limit_bytes=VMEM_GRANT),
        name="adam_update",
    )(grads, adam_m.reshape(view), adam_v.reshape(view))
    return m_new.reshape(adam_m.shape), v_new.reshape(adam_v.shape), sums


def apply_kernel(wide_ranks, group_ref, core_ref, *refs):
    root_refs = refs[: 2 * GROUP]
    grad_hbm, out_hbm, sum_ref, root_buf, grad_buf, out_buf, root_sem, grad_sem, out_sem = refs[
        2 * GROUP :
    ]
    half = root_refs[0].shape[0]
    core = core_ref[0]
    tail = grad_buf.shape[1] - wide_ranks * WIDE * LANES

    def tiles_at(at, tiles):
        return pl.ds(pl.multiple_of(at * LANES, LANES), tiles * LANES)

    def is_wide(rank):
        return (group_ref[1, rank] >= FIRST_WIDE) & (group_ref[1, rank] < NONE)

    def root_copy(step, rank, side):
        at = pl.multiple_of((core if side == 0 else 1 - core) * half, half)
        return pltpu.make_async_copy(
            root_refs[2 * step + side],
            root_buf.at[rank, pl.ds(at, half), :],
            root_sem.at[rank, side],
        )

    def part_copy(source, target, part, sem):
        return pltpu.make_async_copy(source.at[:, part], target.at[:, part], sem)

    def grad_copy(rank):
        part = tiles_at(rank * WIDE, WIDE)
        return part_copy(grad_hbm, grad_buf, part, grad_sem.at[rank])

    def out_copy(rank):
        part = tiles_at(rank * WIDE, WIDE - 1)
        return part_copy(out_buf, out_hbm, part, out_sem.at[rank])

    def single_copy(rank):
        part = tiles_at(rank * WIDE + WIDE - 1, 1)
        return part_copy(out_buf, out_hbm, part, out_sem.at[GROUP + rank])

    def tail_copy(source, target, sem):
        return part_copy(source, target, pl.ds(wide_ranks * WIDE * LANES, tail), sem)

    for rank in range(GROUP):
        if rank < wide_ranks:
            grad_copy(rank).start()
        elif rank == wide_ranks and tail:
            tail_copy(grad_hbm, grad_buf, grad_sem.at[rank]).start()
        for step in range(GROUP):

            @pl.when(group_ref[0, rank] == step)
            def _():
                root_copy(step, rank, 0).start()
                root_copy(step, rank, 1).start()

    def run(rank, part):
        def side(at, total):
            rows = pl.ds(pl.multiple_of(at * half, half), half)
            value = jnp.dot(
                root_buf[rank, rows, :], grad_buf[:, part], preferred_element_type=jnp.float32
            )
            value = value.astype(jnp.bfloat16)
            out_buf[rows, part] = value
            value = value.astype(jnp.float32)
            return total + jnp.sum((value * value).reshape(half // 8, 8, -1), axis=0)

        total = lax.fori_loop(0, 2, side, jnp.zeros((8, part.size), jnp.float32))
        sum_ref[rank] += jnp.sum(total)

    def root_wait(rank):
        root_copy(0, rank, 0).wait()
        root_copy(0, rank, 1).wait()

    def wide(rank, carry):
        grad_copy(rank).wait()
        root_wait(rank)
        sum_ref[rank] = jnp.float32(0.0)

        @pl.when(is_wide(rank))
        def _():
            run(rank, tiles_at(rank * WIDE, WIDE - 1))
            out_copy(rank).start()

        return carry

    lax.fori_loop(0, wide_ranks, wide, 0)
    if tail:
        tail_copy(grad_hbm, grad_buf, grad_sem.at[wide_ranks]).wait()

    def single(rank, carry):
        @pl.when(rank >= wide_ranks)
        def _():
            root_wait(rank)
            sum_ref[rank] = jnp.float32(0.0)

        @pl.when(group_ref[3, rank] == 1)
        def _():
            run(rank, tiles_at(group_ref[2, rank], 1))

        return carry

    lax.fori_loop(0, GROUP, single, 0)
    if tail:
        tail_copy(out_buf, out_hbm, out_sem.at[2 * GROUP]).start()
    for rank in range(wide_ranks):
        single_copy(rank).start()

        @pl.when(jnp.logical_not(is_wide(rank)))
        def _():
            out_copy(rank).start()

    for rank in range(wide_ranks):
        single_copy(rank).wait()
        out_copy(rank).wait()
    if tail:
        tail_copy(out_buf, out_hbm, out_sem.at[2 * GROUP]).wait()


def apply_roots(wide_ranks, group, roots, gathered):
    half, model_rows = roots[0].shape
    cols = gathered.shape[1]
    anywhere = pl.BlockSpec(memory_space=pl.ANY)
    return pl.pallas_call(
        functools.partial(apply_kernel, wide_ranks),
        out_shape=[
            jax.ShapeDtypeStruct((model_rows, cols), jnp.bfloat16),
            jax.ShapeDtypeStruct((GROUP,), jnp.float32),
        ],
        grid_spec=pltpu.PrefetchScalarGridSpec(
            num_scalar_prefetch=2,
            grid=(1,),
            in_specs=[anywhere] * (2 * GROUP + 1),
            out_specs=[anywhere, pl.BlockSpec(memory_space=pltpu.SMEM)],
            scratch_shapes=[
                pltpu.VMEM((GROUP, model_rows, model_rows), jnp.bfloat16),
                pltpu.VMEM((model_rows, cols), jnp.bfloat16),
                pltpu.VMEM((model_rows, cols), jnp.bfloat16),
                pltpu.SemaphoreType.DMA((GROUP, 2)),
                pltpu.SemaphoreType.DMA((GROUP + 1,)),
                pltpu.SemaphoreType.DMA((2 * GROUP + 1,)),
            ],
        ),
        compiler_params=pltpu.CompilerParams(vmem_limit_bytes=VMEM_GRANT),
        name="apply_roots",
    )(*group, *roots, gathered)


def gram_kernel(group_ref, core_ref, mine_ref, other_ref, *refs):
    out_refs = refs[:GROUP]
    keep_buf, send_buf, total_ref, out_sem = refs[GROUP:]
    rank = pl.program_id(0)
    half = keep_buf.shape[1]
    core = core_ref[0]
    step = group_ref[0, rank]
    near = step == 1 + core
    far = step == 2 - core

    total_ref[...] = jnp.zeros(total_ref.shape, jnp.float32)

    def run(tile, tiles):
        columns = pl.ds(pl.multiple_of(tile * LANES, LANES), tiles * LANES)
        rows = pl.ds(pl.multiple_of(core * half, half), half)
        for grad_ref in (mine_ref, other_ref):
            total_ref[...] += lax.dot_general(
                grad_ref[rows, columns],
                grad_ref[:, columns],
                (((1,), (1,)), ((), ())),
                preferred_element_type=jnp.float32,
            )

    @pl.when((group_ref[1, rank] >= FIRST_WIDE) & (group_ref[1, rank] < NONE))
    def _():
        run(rank * WIDE, WIDE - 1)

    @pl.when(group_ref[3, rank] == 1)
    def _():
        run(group_ref[2, rank], 1)

    @pl.when((step == 0) | far)
    def _():
        keep_buf[jnp.minimum(step, 1)] = total_ref[...]

    @pl.when(near | (step == 3))
    def _():
        send_buf[jnp.maximum(step, 2) - 2] = total_ref[...].astype(jnp.bfloat16)

    def out_copy(at):
        source = keep_buf.at[at] if at < 2 else send_buf.at[at - 2]
        return pltpu.make_async_copy(source, out_refs[at], out_sem.at[at])

    @pl.when(step == 0)
    def _():
        out_copy(0).start()

    @pl.when(far)
    def _():
        out_copy(1).start()

    @pl.when(near)
    def _():
        out_copy(2).start()

    @pl.when(step == 3)
    def _():
        out_copy(3).start()

    @pl.when(rank == GROUP - 1)
    def _():
        for at in range(GROUP):
            out_copy(at).wait()


def part_grams(group, mine, other):
    model_rows, cols = mine.shape
    half = model_rows // 2
    whole = pl.BlockSpec((model_rows, cols), lambda r, *_: (0, 0))
    return pl.pallas_call(
        gram_kernel,
        out_shape=[
            jax.ShapeDtypeStruct((half, model_rows), dtype)
            for dtype in (jnp.float32, jnp.float32, jnp.bfloat16, jnp.bfloat16)
        ],
        grid_spec=pltpu.PrefetchScalarGridSpec(
            num_scalar_prefetch=2,
            grid=(GROUP,),
            in_specs=[whole, whole],
            out_specs=[pl.BlockSpec(memory_space=pl.ANY)] * GROUP,
            scratch_shapes=[
                pltpu.VMEM((2, half, model_rows), jnp.float32),
                pltpu.VMEM((2, half, model_rows), jnp.bfloat16),
                pltpu.VMEM((half, model_rows), jnp.float32),
                pltpu.SemaphoreType.DMA((GROUP,)),
            ],
        ),
        compiler_params=pltpu.CompilerParams(vmem_limit_bytes=VMEM_GRANT),
        name="part_grams",
    )(*group, mine, other)


def update_kernel(
    order, base_ref, column_ref, part_ref, scale_ref, weight_ref, back_ref, out_ref, done_ref
):
    layer = pl.program_id(0)
    done_ref[0] = layer
    rows = back_ref.shape[1]
    lane = lax.broadcasted_iota(jnp.int32, (rows, LANES), 1)
    for tile in range(ALL_TILES):
        step = None
        for kind in range(7):
            at = tile - TILE0[kind]
            if not 0 <= at < TILES[kind]:
                continue
            matrix = layer * 7 + kind
            source, column = base_ref[matrix], column_ref[matrix]
            if kind >= FIRST_WIDE:
                source, column = source + chip_at(at // WIDE, order), column + at % WIDE
            elif TILES[kind] > 1:
                source = source + chip_at(at, order)
            else:
                source = source + chip_at(part_ref[matrix], order)
            piece = back_ref[source, :, pl.ds(pl.multiple_of(column * LANES, LANES), LANES)]
            piece = 0.02 * (scale_ref[matrix] * piece.astype(jnp.float32))
            low = STARTS[kind] - tile * LANES
            step = piece if step is None else jnp.where(lane >= low, piece, step)
        where = pl.ds(tile, rows, stride=ALL_TILES)
        out_ref[0, where, :] = weight_ref[0, where, :] - step


def update_weights(order, plan, ratio, weights, returned):
    layers, rows = weights.shape[:2]
    view = (layers, rows * ALL_TILES, LANES)
    flat_spec = pl.BlockSpec((1,) + view[1:], lambda l, *_: (l, 0, 0))
    out, done = pl.pallas_call(
        functools.partial(update_kernel, order),
        out_shape=[
            jax.ShapeDtypeStruct(view, jnp.float32),
            jax.ShapeDtypeStruct((1,), jnp.int32),
        ],
        grid_spec=pltpu.PrefetchScalarGridSpec(
            num_scalar_prefetch=4,
            grid=(layers,),
            in_specs=[flat_spec, pl.BlockSpec(returned.shape, lambda l, *_: (0, 0, 0))],
            out_specs=[flat_spec, pl.BlockSpec(memory_space=pltpu.SMEM)],
        ),
        compiler_params=pltpu.CompilerParams(vmem_limit_bytes=VMEM_GRANT),
        name="update_weights",
    )(plan[5], plan[7], plan[8], ratio.reshape(-1), weights.reshape(view), returned)
    return out.reshape(weights.shape), done


def swap_cores(value):
    return lax.ppermute(value, "tp", [(0, 1), (1, 0)])


def swap_chips(value, step):
    chips = lax.axis_size("fsdp")
    return lax.ppermute(value, "fsdp", [(i, i ^ step) for i in range(chips)])


def hop(value, first, second):
    chips = lax.axis_size("fsdp")
    pairs = [(2 * i, 2 * (i ^ first)) for i in range(chips)]
    pairs += [(2 * i + 1, 2 * (i ^ second) + 1) for i in range(chips)]
    return lax.ppermute(value, ("fsdp", "tp"), pairs)


def refresh(
    wide_ranks,
    shared,
    plan,
    grads,
    weights,
    adam_m,
    adam_v,
    stats,
    roots,
    vec_weight,
    vec_grad,
    vec_m,
    vec_v,
):
    chips = lax.axis_size("fsdp")
    chip = lax.axis_index("fsdp")
    core = lax.axis_index("tp").astype(jnp.int32)
    layers = grads.shape[0]
    rows = grads.shape[1]
    model_rows = rows * chips
    tiles = slot_tiles(wide_ranks, shared)
    cols = tiles * LANES
    order = bit_order(GROUPING, chips)
    steps_to = [chip_at(step, order) for step in range(GROUP)]
    place = place_of(chip, order)
    base = chip - chip_at(place % GROUP, order)
    group = (plan[10], core.reshape(1))

    outgoing = build_send(tiles, order, plan, grads[:, :, 0, :])
    arrived = lax.all_to_all(outgoing, "fsdp", split_axis=0, concat_axis=0, tiled=True)
    along_x = swap_chips(roots[0], steps_to[1])
    along_y = swap_chips(roots[0], steps_to[2])
    along_x, along_y, adam_grads = lax.optimization_barrier((along_x, along_y, grads[:, :, 0, :]))
    adam_m_new, adam_v_new, adam_part = adam_update(adam_grads, adam_m, adam_v)
    forward = jnp.where(core == 0, along_y, along_x)
    across = hop(forward, steps_to[1], steps_to[2])
    across, adam_part = lax.optimization_barrier((across, adam_part))
    group_roots = [along_x, along_y, across]
    all_roots = []
    for part in [roots[0]] + group_roots:
        all_roots += [part, swap_cores(part)]

    arrived, all_roots, adam_part = lax.optimization_barrier((arrived, all_roots, adam_part))
    gathered = arrived.reshape(model_rows, cols)
    precond, sums = apply_roots(wide_ranks, group, all_roots, gathered)
    precond, gathered_other = lax.optimization_barrier((precond, swap_cores(gathered)))
    returned = lax.all_to_all(
        precond.reshape(chips, rows, cols), "fsdp", split_axis=0, concat_axis=0, tiled=True
    )
    ranks = jnp.arange(GROUP, dtype=jnp.int32)
    is_here = (plan[5] == base)[:, None] & (plan[6][:, None] == ranks[None, :])
    shampoo_part = jnp.sum(jnp.where(is_here, sums[None, :], 0.0), axis=1).reshape(layers, 7)
    totals = jnp.stack([adam_part, shampoo_part])
    totals = totals + swap_cores(totals)
    beside = [totals] + [swap_chips(totals, mask) for mask in steps_to[1:]]
    grams = part_grams(group, gathered, gathered_other)
    grams, beside = lax.optimization_barrier((grams, beside))
    totals = sum(beside)
    for bit in order[2:]:
        totals = totals + swap_chips(totals, 1 << bit)
    ratio = jnp.sqrt(totals[0]) / (jnp.sqrt(totals[1]) + 1e-06)
    own_term, far_term, near_term, across_term = grams
    near_term = hop(near_term, steps_to[1], steps_to[2])
    across_term = hop(across_term, steps_to[1], steps_to[2])
    far_term = (far_term + across_term.astype(jnp.float32)).astype(jnp.bfloat16)
    far_term = hop(far_term, steps_to[2], steps_to[1])

    weights_new, done = update_weights(order, plan, ratio, weights, returned)

    stat_term = own_term + near_term.astype(jnp.float32) + far_term.astype(jnp.float32)
    owned = (plan[10][4, 0] == 1) & (done[0] >= 0)
    stats_new = jnp.where(owned, 0.9 * stats[0] + 0.1 * stat_term, stats[0])[None]

    vec_float = vec_grad.astype(jnp.float32)
    vec_m_new = 0.9 * vec_m + 0.1 * vec_float
    vec_v_new = 0.99 * vec_v + 0.01 * vec_float * vec_float
    vec_weight_new = vec_weight - 0.02 * vec_m_new / (jnp.sqrt(vec_v_new) + 1e-08)
    return (weights_new, adam_m_new, adam_v_new, stats_new, vec_weight_new, vec_m_new, vec_v_new)


def on_device(owner, *arrays):
    cases = [(2, 1), (2, 2), (3, 0), (3, 1), (4, 0)]
    plan = make_plan(cases, owner, lax.axis_size("fsdp"))
    branches = [functools.partial(refresh, *case) for case in cases]
    return lax.switch(plan[9][0], branches, plan, *arrays)


def solution(mesh):
    matrix = P(None, "fsdp", "tp", None)
    slot = P("fsdp", "tp", None)
    vector = P(None, ("fsdp", "tp"))
    return jax.shard_map(
        on_device,
        mesh=mesh,
        in_specs=(P(), matrix, matrix, matrix, matrix, slot, slot, vector, vector, vector, vector),
        out_specs=(matrix, matrix, matrix, slot, vector, vector, vector),
        check_vma=False,
    )
```
